32 devices in a mesh: ctx: 8 (over y, x, core), pipe: 4 (over z).
Axes of the slice: x: 2, y: 2, z: 4, core: 2. Of those that a mesh axis runs over, the one named last changes fastest.
Arguments:
- tokens: bfloat16 [1, 1024, 2048], P(None, 'ctx'), may hold values from -6 to 6
- w_qkv: bfloat16 [4, 16, 128, 384], P('pipe'), may hold values from -0.5 to 0.5
- norm_gain: float32 [4, 2048], P('pipe'), may hold values from 0.5 to 1.5
- out_gain: float32 [4, 2048], P('pipe'), may hold values from 0.5 to 1.5
Outputs:
- hidden: bfloat16 [4, 1, 1024, 2048], P('pipe', None, 'ctx')
The draws below stay inside these ranges and needn't reach their ends.
All inputs are finite; a program needn't handle non-finite values.
Results may differ from the reference program's by a relative error of at most 0.03.
Values may be sent and summed in bfloat16 or wider, within the bound.
A program may use at most 128 MiB of HBM per device.

```python
import jax
import jax.numpy as jnp
from jax import lax

HEADS = 16
HEAD_DIM = 128
D = 2048
TOK_DEV = 128
MB = 1
TOKENS = 1024
LAYERS = 4


def levels(rng, dims, pieces, least, largest):
    def one(dim, parts):
        draws = jax.random.uniform(jax.random.fold_in(jax.random.fold_in(rng, 6), dim), (parts,), jnp.float32, least / len(pieces), largest / len(pieces))
        return jnp.repeat(jnp.exp(draws), dims[dim] // parts).reshape((-1,) + (1,) * (len(dims) - dim - 1))

    gain = one(*pieces[0])
    for cut in pieces[1:]:
        gain = gain * one(*cut)
    return gain


def centred(own_key, shape, spread, most, split=(), kind=jnp.bfloat16):
    entries = spread * jax.random.normal(own_key, shape, jnp.float32)
    if split:
        entries = entries * levels(own_key, shape, split, -0.22, 0.18)
    return jnp.clip(entries, -most, most).astype(kind)


def setup_inputs(seed: int = 0) -> dict:
    streams_of = jax.random.split(jax.random.key(seed), 5)
    return {
        "tokens": centred(streams_of[0], (MB, TOKENS, D), 1.0, 6.0, ((1, 8),)),
        "w_qkv": centred(streams_of[1], (LAYERS, HEADS, HEAD_DIM, 3 * HEAD_DIM), HEAD_DIM ** -0.5, 0.5, ((0, 4),)),
        "norm_gain": jnp.clip(0.5 + 1.0 * jax.random.uniform(streams_of[2], (LAYERS, D), jnp.float32) ** levels(streams_of[2], (LAYERS, D), ((0, 4),), -0.2, 0.2), 0.5, 1.5),
        "out_gain": jnp.clip(0.5 + 1.0 * jax.random.uniform(streams_of[3], (LAYERS, D), jnp.float32) ** levels(streams_of[3], (LAYERS, D), ((0, 4),), -0.2, 0.2), 0.5, 1.5),
    }


epsilon = 1e-06

def rounded(value):
    return lax.optimization_barrier(value.astype(jnp.bfloat16)).astype(jnp.float32)

def one_layer(stream, gain_in, weights, gain_out):
    length = stream.shape[0]
    head_count = weights.shape[0]
    head_dim = weights.shape[1]
    widened = stream.astype(jnp.float32)
    normed = rounded(widened * lax.rsqrt(lax.optimization_barrier(jnp.mean(widened * widened, -1, keepdims=True)) + epsilon) * gain_in)
    projected = jnp.einsum('thd,hde->hte', normed.reshape(length, head_count, head_dim), weights.astype(jnp.float32))
    queries = rounded(projected[..., :head_dim] * head_dim ** (-0.5))
    keys_all = rounded(projected[..., head_dim:2 * head_dim])
    values_all = rounded(projected[..., 2 * head_dim:])
    blocks = length // TOK_DEV
    query_blocks = queries.reshape(head_count, blocks, TOK_DEV, head_dim)
    key_blocks = keys_all.reshape(head_count, blocks, TOK_DEV, head_dim)
    value_blocks = values_all.reshape(head_count, blocks, TOK_DEV, head_dim)
    kv_state = jnp.einsum('hbte,hbtf->hbef', key_blocks, value_blocks)
    running = jnp.cumsum(kv_state, axis=1)
    prefix = jnp.concatenate([jnp.zeros((head_count, 1, head_dim, head_dim), jnp.float32), running[:, :-1]], axis=1)
    prefix = rounded(prefix)
    scores = jnp.einsum('hbte,hbse->hbts', query_blocks, key_blocks)
    positions = jnp.arange(TOK_DEV, dtype=jnp.int32)
    causal = positions[:, None] >= positions[None, :]
    masked = rounded(jnp.where(causal, scores, 0.0))
    mixed_heads = jnp.einsum('hbts,hbsf->hbtf', masked, value_blocks) + jnp.einsum('hbte,hbef->hbtf', query_blocks, prefix)
    mixed_heads = mixed_heads * lax.rsqrt(lax.optimization_barrier(jnp.mean(mixed_heads * mixed_heads, -1, keepdims=True)) + epsilon)
    branch = jnp.transpose(mixed_heads.reshape(head_count, length, head_dim), (1, 0, 2)).reshape(length, head_count * head_dim)
    return (widened + branch * gain_out).astype(jnp.bfloat16)

def reference(tokens, w_qkv, norm_gain, out_gain):
    layer_outputs = []
    for layer_index in range(LAYERS):
        sequence_outputs = []
        for sequence_index in range(MB):
            stream = tokens[sequence_index] if layer_index == 0 else layer_outputs[-1][sequence_index]
            sequence_outputs.append(one_layer(stream, norm_gain[layer_index], w_qkv[layer_index], out_gain[layer_index]))
        layer_outputs.append(jnp.stack(sequence_outputs, 0))
    return jnp.stack(layer_outputs, 0)
```

```python
import functools

import jax
import jax.numpy as jnp
from jax import lax
from jax.experimental import pallas as pl
from jax.experimental.pallas import tpu as pltpu
from jax.sharding import PartitionSpec as P

epsilon = 1e-06


def shifted(block, axis, distance):
    devices = range(lax.axis_size(axis))
    route = [(i - distance, i) for i in devices if i - distance in devices]
    return lax.ppermute(block, axis, route)


def run_layer(stream, gain_in, weights, gain_out):
    row_count = stream.shape[0]
    head_count = weights.shape[0]
    head_dim = weights.shape[1]
    widened = stream.astype(jnp.float32)
    normed = (
        widened * lax.rsqrt(jnp.mean(widened * widened, -1, keepdims=True) + epsilon) * gain_in
    ).astype(jnp.bfloat16)
    projected = jnp.einsum(
        "thd,hde->hte",
        normed.reshape(row_count, head_count, head_dim),
        weights,
        preferred_element_type=jnp.float32,
    )
    queries = (projected[..., :head_dim] * head_dim ** (-0.5)).astype(jnp.bfloat16)
    keys_local = projected[..., head_dim : 2 * head_dim].astype(jnp.bfloat16)
    values_local = projected[..., 2 * head_dim :].astype(jnp.bfloat16)
    kv_state = jnp.einsum(
        "hte,htf->hef", keys_local, values_local, preferred_element_type=jnp.float32
    )
    flat_state = kv_state.reshape(1, head_count * head_dim, head_dim)
    spread = lax.all_to_all(
        flat_state.astype(jnp.bfloat16), "ctx", split_axis=1, concat_axis=0, tiled=True
    ).astype(flat_state.dtype)
    running = jnp.cumsum(spread, axis=0)
    lower = jnp.concatenate([jnp.zeros_like(spread[:1]), running[:-1]], axis=0)
    returned = lax.all_to_all(
        lower.astype(jnp.bfloat16), "ctx", split_axis=0, concat_axis=1, tiled=True
    ).astype(lower.dtype)
    prefix = returned.reshape(kv_state.shape)
    scores = jnp.einsum("hte,hse->hts", queries, keys_local, preferred_element_type=jnp.float32)
    positions = jnp.arange(row_count, dtype=jnp.int32)
    causal = positions[:, None] >= positions[None, :]
    masked = jnp.where(causal, scores, 0.0).astype(jnp.bfloat16)
    mixed_heads = jnp.einsum(
        "hts,hsf->htf", masked, values_local, preferred_element_type=jnp.float32
    )
    mixed_heads = mixed_heads + jnp.einsum(
        "hte,hef->htf", queries, prefix.astype(jnp.bfloat16), preferred_element_type=jnp.float32
    )
    mixed_heads = mixed_heads * lax.rsqrt(
        jnp.mean(mixed_heads * mixed_heads, -1, keepdims=True) + epsilon
    )
    branch = jnp.transpose(mixed_heads, (1, 0, 2)).reshape(row_count, head_count * head_dim)
    return (widened + branch * gain_out).astype(jnp.bfloat16)


def shards(tokens, w_qkv, norm_gain, out_gain):
    section_count = lax.axis_size("pipe")
    section_index = lax.axis_index("pipe")
    micro_count = tokens.shape[0]
    hidden_buffer = jnp.zeros(tokens.shape, jnp.bfloat16)
    carried = jnp.zeros(tokens.shape[1:], jnp.bfloat16)
    total_steps = micro_count + section_count - 1
    for tick_index in range(total_steps):
        fresh = tokens[min(tick_index, micro_count - 1)]
        layer_input = jnp.where(section_index == 0, fresh, carried)
        result = run_layer(layer_input, norm_gain[0], w_qkv[0], out_gain[0])
        micro_index = tick_index - section_index
        usable = (micro_index >= 0) & (micro_index < micro_count)
        slot_index = jnp.clip(micro_index, 0, micro_count - 1)
        previous = lax.dynamic_index_in_dim(hidden_buffer, slot_index, 0, keepdims=False)
        hidden_buffer = lax.dynamic_update_index_in_dim(
            hidden_buffer, jnp.where(usable, result, previous), slot_index, 0
        )
        if tick_index + 1 < total_steps:
            carried = shifted(result, "pipe", 1)
    return hidden_buffer[None]


MESH = pl.DeviceIdType.MESH
FAR_FIRST = (6, 7, 2, 4, 3, 5, 1)


def partner(index, flips):
    total = 0
    for bit in (1, 2, 4):
        own = lax.rem(index // bit, 2)
        total = total + (lax.rem(own + 1, 2) if flips & bit else own) * bit
    return total


def lanes_to_rows(row):
    return jnp.broadcast_to(row, (128, row.shape[1])).T


def product(a, b):
    return jnp.dot(a, b, preferred_element_type=jnp.float32)


GROUPS = 2


def relay_kernel(
    sizes,
    tok_ref,
    w_ref,
    gin_ref,
    gout_ref,
    out_ref,
    own,
    stream,
    turned,
    raw,
    gain_in,
    weights,
    gains,
    gain_cols,
    left,
    right,
    state,
    squares,
    local_sem,
    tok_send,
    tok_recv,
    sq_send,
    sq_recv,
    w_send,
    w_recv,
    out_send,
    out_recv,
):
    ctx_size, sections, heads, dim, tokens = sizes
    width = heads * dim
    features = ctx_size * width
    span = ctx_size // GROUPS
    last = sections - 1
    c = lax.axis_index("ctx")
    z = lax.axis_index("pipe")

    def cols(device):
        return pl.ds(pl.multiple_of(device * width, width), width)

    def rows(device):
        return pl.ds(pl.multiple_of(device * tokens, tokens), tokens)

    local = [
        pltpu.make_async_copy(tok_ref.at[0], own, local_sem.at[0]),
        pltpu.make_async_copy(w_ref.at[0, pl.ds(c * heads, heads)], raw, local_sem.at[1]),
        pltpu.make_async_copy(gin_ref.at[:, cols(c)], gain_in, local_sem.at[2]),
        pltpu.make_async_copy(gout_ref.at[:, cols(c)], gains.at[z], local_sem.at[3]),
        pltpu.make_async_copy(tok_ref.at[0, :, cols(c)], stream.at[rows(c)], local_sem.at[4]),
    ]
    for copy in local:
        copy.start()

    barrier = pltpu.get_barrier_semaphore()
    for d in FAR_FIRST:
        pl.semaphore_signal(barrier, 1, device_id=(partner(c, d), z), device_id_type=MESH)
    for step in range(1, sections):
        other = lax.rem(z + step, sections)
        pl.semaphore_signal(barrier, 1, device_id=(c, other), device_id_type=MESH)

    def fold():
        for copy in local[1:4]:
            copy.wait()
        for h in range(heads):
            across = gain_in[:, h * dim : (h + 1) * dim]
            query = raw[h, :, :dim]
            key = raw[h, :, dim : 2 * dim]
            value = raw[h, :, 2 * dim :].astype(jnp.float32)
            crossed = lax.dot_general(
                key, query, (((1,), (1,)), ((), ())), preferred_element_type=jnp.float32
            )
            crossed = crossed * (across * dim ** (-0.5)) * lanes_to_rows(across)
            weights[z, h, :dim] = crossed.astype(jnp.bfloat16)
            weights[z, h, dim:] = (value.T * across).astype(jnp.bfloat16)

    @pl.when(z == 0)
    def _():
        fold()

    pl.semaphore_wait(barrier, ctx_size + sections - 2)

    def tok_copy(d):
        to = partner(c, d)
        return pltpu.make_async_remote_copy(
            tok_ref.at[0, :, cols(to)], stream.at[rows(c)],
            tok_send.at[d], tok_recv.at[d], device_id=(to, z), device_id_type=MESH,
        )

    def tok_arrival(block):
        d = partner(c, block)
        return pltpu.make_async_remote_copy(
            tok_ref.at[0, :, cols(block)], stream.at[rows(block)],
            tok_send.at[d], tok_recv.at[d], device_id=(block, z), device_id_type=MESH,
        )

    def part(g):
        return pl.ds(g * span, span)

    def sq_copy(layer, g, d):
        return pltpu.make_async_remote_copy(
            squares.at[layer, c, part(g)], squares.at[layer, c, part(g)],
            sq_send.at[layer, g], sq_recv.at[layer, g],
            device_id=(partner(c, d), z), device_id_type=MESH,
        )

    def sq_wait(sem, layer, g):
        every = squares.at[layer, pl.ds(0, ctx_size - 1), part(g)]
        pltpu.make_async_copy(every, every, sem.at[layer, g]).wait()

    def w_copies(layer, to, slot):
        pieces = [weights.at[layer, h] for h in range(heads)] + [gains.at[layer]]
        return [
            pltpu.make_async_remote_copy(
                piece, piece, w_send.at[slot, i], w_recv.at[layer, i],
                device_id=(c, to), device_id_type=MESH,
            )
            for i, piece in enumerate(pieces)
        ]

    def send_weights(layer, to):
        for copy in w_copies(layer, to, to):
            copy.start()

    def weights_sent(layer, to):
        for copy in w_copies(layer, to, to):
            copy.wait_send()

    @pl.when(z == 0)
    def _():
        send_weights(0, last)

    for d in FAR_FIRST:
        tok_copy(d).start()

    local[0].wait()
    folded = jnp.zeros((tokens, 128), jnp.float32)
    for i in range(features // 128):
        piece = own[:, i * 128 : (i + 1) * 128].astype(jnp.float32)
        folded = folded + piece * piece
    total = jnp.sum(folded.T, 0, keepdims=True)
    which = lax.broadcasted_iota(jnp.int32, (ctx_size, tokens), 0)
    squares[0, c] = jnp.where(which == c, jnp.broadcast_to(total, (ctx_size, tokens)), 0.0)
    for g in range(GROUPS):
        for d in FAR_FIRST:
            sq_copy(0, g, d).start()

    @pl.when(z > 0)
    def _():
        fold()

    @pl.when(z == 0)
    def _():
        weights_sent(0, last)
        for to in range(last - 1, 0, -1):
            send_weights(0, to)

    for layer in range(1, last):
        @pl.when(z == layer)
        def _():
            send_weights(layer, last)

    def await_weights(layer):
        for copy in w_copies(layer, z, 0):
            copy.wait_recv()

    at_row = lax.broadcasted_iota(jnp.int32, (tokens, tokens), 0)
    at_col = lax.broadcasted_iota(jnp.int32, (tokens, tokens), 1)
    causal = at_row <= at_col

    def out_copy(block):
        return pltpu.make_async_remote_copy(
            stream.at[rows(block)], out_ref.at[0, 0, :, cols(c)],
            out_send.at[block], out_recv.at[c], device_id=(block, z), device_id_type=MESH,
        )

    def own_out():
        return pltpu.make_async_copy(
            stream.at[rows(c)], out_ref.at[0, 0, :, cols(c)], local_sem.at[0]
        )

    def project(layer, pair):
        lanes = slice(pair * 2 * tokens, (pair + 1) * 2 * tokens)
        for h in range(heads):
            mine = slice(h * dim, (h + 1) * dim)
            projected = product(weights[layer, h], turned[h, :, lanes])
            queries = projected[:dim].astype(jnp.bfloat16)
            right[h, tokens:, lanes] = queries
            left[h, :, lanes] = projected[dim:]
            for i in range(2):
                here = slice((pair * 2 + i) * tokens, (pair * 2 + i + 1) * tokens)
                scores = product(stream[here, mine], queries[:, i * tokens : (i + 1) * tokens])
                right[h, :tokens, here] = jnp.where(causal, scores, 0.0).astype(jnp.bfloat16)

    def spread_gains(layer):
        for h in range(heads):
            gain_cols[h] = lanes_to_rows(gains[layer, :, h * dim : (h + 1) * dim])

    def mix(layer, g):
        sq_wait(sq_recv, layer, g)
        mean = jnp.sum(squares[layer, :, g * span : (g + 1) * span], 0) * (1.0 / features)
        scale = lax.rsqrt(mean + epsilon)
        twice = scale * scale
        sums = []
        running = [state[h] if g else jnp.zeros((dim, dim), jnp.float32) for h in range(heads)]
        for i in range(span):
            block = g * span + i
            here = slice(block * tokens, (block + 1) * tokens)
            own_scale, own_twice = scale[i : i + 1], twice[i : i + 1]
            folded = jnp.zeros((1, tokens), jnp.float32)
            for h in range(heads):
                mine = slice(h * dim, (h + 1) * dim)
                scaled = (left[h, :, here] * own_twice).astype(jnp.bfloat16)
                mixed = product(
                    jnp.concatenate([scaled, running[h].astype(jnp.bfloat16)], 1),
                    right[h, :, here],
                )
                if block + 1 < ctx_size:
                    running[h] = running[h] + product(scaled, stream[here, mine])
                power = jnp.sum(mixed * mixed, 0, keepdims=True) * (1.0 / dim)
                factor = own_scale * lax.rsqrt(own_twice * power + epsilon)
                entering = turned[h, :, here].astype(jnp.float32)
                leaving = entering + gain_cols[h] * (mixed * factor)
                rounded = leaving.astype(jnp.bfloat16)
                turned[h, :, here] = rounded
                stream[here, mine] = rounded.T
                folded = folded + jnp.sum(leaving * leaving, 0, keepdims=True)
            sums.append(folded)
        if g + 1 < GROUPS:
            for h in range(heads):
                state[h] = running[h]
        squares[layer + 1, c, g * span : (g + 1) * span] = jnp.concatenate(sums, 0)

        @pl.when(layer < z)
        def _():
            for d in FAR_FIRST:
                sq_copy(layer + 1, g, d).start()

        @pl.when(layer == z)
        def _():
            for i in range(span):
                block = g * span + i

                @pl.when(c != block)
                def _():
                    out_copy(block).start()

                @pl.when(c == block)
                def _():
                    own_out().start()

    @pl.when(z > 0)
    def _():
        await_weights(0)

    spread_gains(0)
    for pair in range(ctx_size // 2):
        for block in (pair * 2, pair * 2 + 1):
            @pl.when(c != block)
            def _():
                tok_arrival(block).wait_recv()

            @pl.when(c == block)
            def _():
                local[4].wait()

        for block in (pair * 2, pair * 2 + 1):
            here = slice(block * tokens, (block + 1) * tokens)
            for h in range(heads):
                turned[h, :, here] = stream[here, h * dim : (h + 1) * dim].T
        project(0, pair)

    for layer in range(1, last - 1):
        @pl.when(z == layer)
        def _():
            for to in range(last - 1, layer, -1):
                send_weights(layer, to)

    def one_layer(layer, carry):
        for g in range(GROUPS):
            mix(layer, g)

        @pl.when(layer < z)
        def _():
            @pl.when(layer + 1 < z)
            def _():
                await_weights(layer + 1)

            spread_gains(layer + 1)
            for pair in range(ctx_size // 2):
                project(layer + 1, pair)

        for g in range(GROUPS):
            sq_wait(sq_send, layer, g)
        return carry

    lax.fori_loop(0, z + 1, one_layer, 0)

    own_out().wait()
    for d in FAR_FIRST:
        tok_copy(d).wait_send()
    for d in FAR_FIRST:
        to = partner(c, d)
        pltpu.make_async_remote_copy(
            stream.at[rows(to)], out_ref.at[0, 0, :, cols(c)],
            out_send.at[to], out_recv.at[to], device_id=(to, z), device_id_type=MESH,
        ).wait()

    @pl.when(z == 0)
    def _():
        for to in range(1, last):
            weights_sent(0, to)

    for layer in range(1, last):
        @pl.when(z == layer)
        def _():
            for to in range(layer + 1, sections):
                weights_sent(layer, to)


def relay(tokens, w_qkv, norm_gain, out_gain):
    ctx_size, sections = lax.axis_size("ctx"), lax.axis_size("pipe")
    rows, features = tokens.shape[1:]
    all_heads, dim = w_qkv.shape[1:3]
    heads = all_heads // ctx_size
    width = heads * dim
    length = ctx_size * rows
    dma = pltpu.SemaphoreType.DMA
    return pl.pallas_call(
        functools.partial(relay_kernel, (ctx_size, sections, heads, dim, rows)),
        out_shape=jax.ShapeDtypeStruct((1,) + tokens.shape, jnp.bfloat16),
        in_specs=[pl.BlockSpec(memory_space=pl.ANY)] * 4,
        out_specs=pl.BlockSpec(memory_space=pl.ANY),
        scratch_shapes=[
            pltpu.VMEM((rows, features), jnp.bfloat16),
            pltpu.VMEM((length, width), jnp.bfloat16),
            pltpu.VMEM((heads, dim, length), jnp.bfloat16),
            pltpu.VMEM((heads, dim, 3 * dim), jnp.bfloat16),
            pltpu.VMEM((1, width), jnp.float32),
            pltpu.VMEM((sections, heads, 2 * dim, dim), jnp.bfloat16),
            pltpu.VMEM((sections, 1, width), jnp.float32),
            pltpu.VMEM((heads, dim, rows), jnp.float32),
            pltpu.VMEM((heads, dim, length), jnp.float32),
            pltpu.VMEM((heads, rows + dim, length), jnp.bfloat16),
            pltpu.VMEM((heads, dim, dim), jnp.float32),
            pltpu.VMEM((sections + 1, ctx_size, ctx_size, rows), jnp.float32),
            dma((5,)),
            dma((ctx_size,)),
            dma((ctx_size,)),
            dma((sections, GROUPS)),
            dma((sections, GROUPS)),
            dma((sections, heads + 1)),
            dma((sections, heads + 1)),
            dma((ctx_size,)),
            dma((ctx_size,)),
        ],
        compiler_params=pltpu.CompilerParams(collective_id=0, has_side_effects=True),
    )(tokens, w_qkv, norm_gain, out_gain)


def solution(mesh):
    ctx_size, sections = mesh.shape["ctx"], mesh.shape["pipe"]

    def body(tokens, w_qkv, norm_gain, out_gain):
        micro_count, rows = tokens.shape[:2]
        fits = (
            ctx_size == 8
            and sections == 4
            and micro_count == 1
            and rows == 128
            and w_qkv.shape[1] == 2 * ctx_size
            and w_qkv.shape[2] == 128
        )
        return (relay if fits else shards)(tokens, w_qkv, norm_gain, out_gain)

    placed = (P(None, "ctx", None), P("pipe", None, None, None), P("pipe", None), P("pipe", None))
    return jax.shard_map(
        body, mesh=mesh, in_specs=placed, out_specs=P("pipe", None, "ctx", None), check_vma=False
    )
```

```python
import functools

import jax
import jax.numpy as jnp
from jax import lax
from jax.experimental import pallas as pl
from jax.experimental.pallas import tpu as pltpu
from jax.sharding import PartitionSpec as P

epsilon = 1e-06


def shifted(block, axis, distance):
    devices = range(lax.axis_size(axis))
    route = [(i - distance, i) for i in devices if i - distance in devices]
    return lax.ppermute(block, axis, route)


def run_layer(stream, gain_in, weights, gain_out):
    row_count = stream.shape[0]
    head_count = weights.shape[0]
    head_dim = weights.shape[1]
    widened = stream.astype(jnp.float32)
    normed = (
        widened * lax.rsqrt(jnp.mean(widened * widened, -1, keepdims=True) + epsilon) * gain_in
    ).astype(jnp.bfloat16)
    projected = jnp.einsum(
        "thd,hde->hte",
        normed.reshape(row_count, head_count, head_dim),
        weights,
        preferred_element_type=jnp.float32,
    )
    queries = (projected[..., :head_dim] * head_dim ** (-0.5)).astype(jnp.bfloat16)
    keys_local = projected[..., head_dim : 2 * head_dim].astype(jnp.bfloat16)
    values_local = projected[..., 2 * head_dim :].astype(jnp.bfloat16)
    kv_state = jnp.einsum(
        "hte,htf->hef", keys_local, values_local, preferred_element_type=jnp.float32
    )
    flat_state = kv_state.reshape(1, head_count * head_dim, head_dim)
    spread = lax.all_to_all(
        flat_state.astype(jnp.bfloat16), "ctx", split_axis=1, concat_axis=0, tiled=True
    ).astype(flat_state.dtype)
    running = jnp.cumsum(spread, axis=0)
    lower = jnp.concatenate([jnp.zeros_like(spread[:1]), running[:-1]], axis=0)
    returned = lax.all_to_all(
        lower.astype(jnp.bfloat16), "ctx", split_axis=0, concat_axis=1, tiled=True
    ).astype(lower.dtype)
    prefix = returned.reshape(kv_state.shape)
    scores = jnp.einsum("hte,hse->hts", queries, keys_local, preferred_element_type=jnp.float32)
    positions = jnp.arange(row_count, dtype=jnp.int32)
    causal = positions[:, None] >= positions[None, :]
    masked = jnp.where(causal, scores, 0.0).astype(jnp.bfloat16)
    mixed_heads = jnp.einsum(
        "hts,hsf->htf", masked, values_local, preferred_element_type=jnp.float32
    )
    mixed_heads = mixed_heads + jnp.einsum(
        "hte,hef->htf", queries, prefix.astype(jnp.bfloat16), preferred_element_type=jnp.float32
    )
    mixed_heads = mixed_heads * lax.rsqrt(
        jnp.mean(mixed_heads * mixed_heads, -1, keepdims=True) + epsilon
    )
    branch = jnp.transpose(mixed_heads, (1, 0, 2)).reshape(row_count, head_count * head_dim)
    return (widened + branch * gain_out).astype(jnp.bfloat16)


def shards(tokens, w_qkv, norm_gain, out_gain):
    section_count = lax.axis_size("pipe")
    section_index = lax.axis_index("pipe")
    micro_count = tokens.shape[0]
    hidden_buffer = jnp.zeros(tokens.shape, jnp.bfloat16)
    carried = jnp.zeros(tokens.shape[1:], jnp.bfloat16)
    total_steps = micro_count + section_count - 1
    for tick_index in range(total_steps):
        fresh = tokens[min(tick_index, micro_count - 1)]
        layer_input = jnp.where(section_index == 0, fresh, carried)
        result = run_layer(layer_input, norm_gain[0], w_qkv[0], out_gain[0])
        micro_index = tick_index - section_index
        usable = (micro_index >= 0) & (micro_index < micro_count)
        slot_index = jnp.clip(micro_index, 0, micro_count - 1)
        previous = lax.dynamic_index_in_dim(hidden_buffer, slot_index, 0, keepdims=False)
        hidden_buffer = lax.dynamic_update_index_in_dim(
            hidden_buffer, jnp.where(usable, result, previous), slot_index, 0
        )
        if tick_index + 1 < total_steps:
            carried = shifted(result, "pipe", 1)
    return hidden_buffer[None]


MESH = pl.DeviceIdType.MESH
FAR_FIRST = (6, 7, 2, 4, 3, 5, 1)


def partner(index, flips):
    total = 0
    for bit in (1, 2, 4):
        own = lax.rem(index // bit, 2)
        total = total + (lax.rem(own + 1, 2) if flips & bit else own) * bit
    return total


def lanes_to_rows(row):
    return jnp.broadcast_to(row, (128, row.shape[1])).T


def product(a, b):
    return jnp.dot(a, b, preferred_element_type=jnp.float32)


GROUPS = 2


def relay_kernel(
    sizes,
    tok_ref,
    w_ref,
    gin_ref,
    gout_ref,
    out_ref,
    own,
    stream,
    turned,
    raw,
    gain_in,
    weights,
    gains,
    gain_cols,
    left,
    right,
    state,
    squares,
    local_sem,
    tok_send,
    tok_recv,
    sq_send,
    sq_recv,
    w_send,
    w_recv,
    out_send,
    out_recv,
):
    ctx_size, sections, heads, dim, tokens = sizes
    width = heads * dim
    features = ctx_size * width
    span = ctx_size // GROUPS
    last = sections - 1
    c = lax.axis_index("ctx")
    z = lax.axis_index("pipe")

    def cols(device):
        return pl.ds(pl.multiple_of(device * width, width), width)

    def rows(device):
        return pl.ds(pl.multiple_of(device * tokens, tokens), tokens)

    local = [
        pltpu.make_async_copy(tok_ref.at[0], own, local_sem.at[0]),
        pltpu.make_async_copy(w_ref.at[0, pl.ds(c * heads, heads)], raw, local_sem.at[1]),
        pltpu.make_async_copy(gin_ref.at[:, cols(c)], gain_in, local_sem.at[2]),
        pltpu.make_async_copy(gout_ref.at[:, cols(c)], gains.at[z], local_sem.at[3]),
        pltpu.make_async_copy(tok_ref.at[0, :, cols(c)], stream.at[rows(c)], local_sem.at[4]),
    ]
    for copy in local:
        copy.start()

    barrier = pltpu.get_barrier_semaphore()
    for d in FAR_FIRST:
        pl.semaphore_signal(barrier, 1, device_id=(partner(c, d), z), device_id_type=MESH)
    for step in range(1, sections):
        other = lax.rem(z + step, sections)
        pl.semaphore_signal(barrier, 1, device_id=(c, other), device_id_type=MESH)

    def fold():
        for copy in local[1:4]:
            copy.wait()
        for h in range(heads):
            across = gain_in[:, h * dim : (h + 1) * dim]
            query = raw[h, :, :dim]
            key = raw[h, :, dim : 2 * dim]
            value = raw[h, :, 2 * dim :].astype(jnp.float32)
            crossed = lax.dot_general(
                key, query, (((1,), (1,)), ((), ())), preferred_element_type=jnp.float32
            )
            crossed = crossed * (across * dim ** (-0.5)) * lanes_to_rows(across)
            weights[z, h, :dim] = crossed.astype(jnp.bfloat16)
            weights[z, h, dim:] = (value.T * across).astype(jnp.bfloat16)

    @pl.when(z == 0)
    def _():
        fold()

    pl.semaphore_wait(barrier, ctx_size + sections - 2)

    def tok_copy(d):
        to = partner(c, d)
        return pltpu.make_async_remote_copy(
            tok_ref.at[0, :, cols(to)], stream.at[rows(c)],
            tok_send.at[d], tok_recv.at[d], device_id=(to, z), device_id_type=MESH,
        )

    def part(g):
        return pl.ds(g * span, span)

    def sq_copy(layer, g, d):
        return pltpu.make_async_remote_copy(
            squares.at[layer, c, part(g)], squares.at[layer, c, part(g)],
            sq_send.at[layer, g], sq_recv.at[layer, g],
            device_id=(partner(c, d), z), device_id_type=MESH,
        )

    def sq_wait(sem, layer, g):
        every = squares.at[layer, pl.ds(0, ctx_size - 1), part(g)]
        pltpu.make_async_copy(every, every, sem.at[layer, g]).wait()

    def w_copies(layer, to, slot):
        pieces = [weights.at[layer, h] for h in range(heads)] + [gains.at[layer]]
        return [
            pltpu.make_async_remote_copy(
                piece, piece, w_send.at[slot, i], w_recv.at[layer, i],
                device_id=(c, to), device_id_type=MESH,
            )
            for i, piece in enumerate(pieces)
        ]

    def send_weights(layer, to):
        for copy in w_copies(layer, to, to):
            copy.start()

    def weights_sent(layer, to):
        for copy in w_copies(layer, to, to):
            copy.wait_send()

    @pl.when(z == 0)
    def _():
        send_weights(0, last)

    for d in FAR_FIRST:
        tok_copy(d).start()

    local[0].wait()
    folded = jnp.zeros((tokens, 128), jnp.float32)
    for i in range(features // 128):
        piece = own[:, i * 128 : (i + 1) * 128].astype(jnp.float32)
        folded = folded + piece * piece
    total = jnp.sum(folded.T, 0, keepdims=True)
    which = lax.broadcasted_iota(jnp.int32, (ctx_size, tokens), 0)
    squares[0, c] = jnp.where(which == c, jnp.broadcast_to(total, (ctx_size, tokens)), 0.0)
    for g in range(GROUPS):
        for d in FAR_FIRST:
            sq_copy(0, g, d).start()

    @pl.when(z > 0)
    def _():
        fold()

    def await_weights(layer):
        for copy in w_copies(layer, z, 0):
            copy.wait_recv()

    at_row = lax.broadcasted_iota(jnp.int32, (tokens, tokens), 0)
    at_col = lax.broadcasted_iota(jnp.int32, (tokens, tokens), 1)
    causal = at_row <= at_col

    def out_copy(block):
        return pltpu.make_async_remote_copy(
            stream.at[rows(block)], out_ref.at[0, 0, :, cols(c)],
            out_send.at[block], out_recv.at[c], device_id=(block, z), device_id_type=MESH,
        )

    def own_out():
        return pltpu.make_async_copy(
            stream.at[rows(c)], out_ref.at[0, 0, :, cols(c)], local_sem.at[0]
        )

    def attend(h, block, projected):
        queries = projected[:dim].astype(jnp.bfloat16)
        right[h, block, tokens:] = queries
        left[h, block] = projected[dim:]
        scores = product(stream[rows(block), h * dim : (h + 1) * dim], queries)
        right[h, block, :tokens] = jnp.where(causal, scores, 0.0).astype(jnp.bfloat16)

    def project(layer, pair):
        for h in range(heads):
            both = jnp.concatenate([turned[h, 2 * pair], turned[h, 2 * pair + 1]], 1)
            projected = product(weights[layer, h], both)
            for i in range(2):
                attend(h, 2 * pair + i, projected[:, i * tokens : (i + 1) * tokens])

    def project_first(block):
        for h in range(heads):
            entering = stream[rows(block), h * dim : (h + 1) * dim].T
            turned[h, block] = entering
            attend(h, block, product(weights[0, h], entering))

    def spread_gains(layer):
        for h in range(heads):
            gain_cols[h] = lanes_to_rows(gains[layer, :, h * dim : (h + 1) * dim])

    def mix(layer, g):
        sq_wait(sq_recv, layer, g)
        mean = jnp.sum(squares[layer, :, g * span : (g + 1) * span], 0) * (1.0 / features)
        scale = lax.rsqrt(mean + epsilon)
        twice = scale * scale
        sums = []
        running = [state[h] if g else jnp.zeros((dim, dim), jnp.float32) for h in range(heads)]
        for i in range(span):
            block = g * span + i
            here = slice(block * tokens, (block + 1) * tokens)
            own_scale, own_twice = scale[i : i + 1], twice[i : i + 1]
            folded = jnp.zeros((1, tokens), jnp.float32)
            for h in range(heads):
                mine = slice(h * dim, (h + 1) * dim)
                scaled = (left[h, block] * own_twice).astype(jnp.bfloat16)
                mixed = product(
                    jnp.concatenate([scaled, running[h].astype(jnp.bfloat16)], 1),
                    right[h, block],
                )
                if block + 1 < ctx_size:
                    running[h] = running[h] + product(scaled, stream[here, mine])
                power = jnp.sum(mixed * mixed, 0, keepdims=True) * (1.0 / dim)
                factor = own_scale * lax.rsqrt(own_twice * power + epsilon)
                entering = turned[h, block].astype(jnp.float32)
                leaving = entering + gain_cols[h] * (mixed * factor)
                rounded = leaving.astype(jnp.bfloat16)
                turned[h, block] = rounded
                stream[here, mine] = rounded.T
                folded = folded + jnp.sum(leaving * leaving, 0, keepdims=True)
            sums.append(folded)
        if g + 1 < GROUPS:
            for h in range(heads):
                state[h] = running[h]
        squares[layer + 1, c, g * span : (g + 1) * span] = jnp.concatenate(sums, 0)

        @pl.when(layer < z)
        def _():
            for d in FAR_FIRST:
                sq_copy(layer + 1, g, d).start()

        @pl.when(layer == z)
        def _():
            for i in range(span):
                block = g * span + i

                @pl.when(c != block)
                def _():
                    out_copy(block).start()

                @pl.when(c == block)
                def _():
                    own_out().start()

    @pl.when(z == 0)
    def _():
        weights_sent(0, last)
        send_weights(0, last - 1)

    inner = jnp.logical_and(z > 0, z < last)

    @pl.when(inner)
    def _():
        for d in (6, 7):
            tok_copy(d).wait_recv()
        for layer in range(1, last - 1):
            @pl.when(z == layer)
            def _():
                send_weights(layer, last)
                weights_sent(layer, last)
                for to in range(last - 1, layer, -1):
                    send_weights(layer, to)

    @pl.when(z > 0)
    def _():
        await_weights(0)

    @pl.when(z == last - 1)
    def _():
        for to in range(1, last - 1):
            send_weights(0, to)

    spread_gains(0)
    local[4].wait()
    project_first(c)
    for pair in ((1,), (6, 7), (2, 4), (3, 5)):
        if pair == (6, 7):
            @pl.when(jnp.logical_not(inner))
            def _():
                for d in pair:
                    tok_copy(d).wait_recv()
        else:
            for d in pair:
                tok_copy(d).wait_recv()
        for d in pair:
            project_first(partner(c, d))

    @pl.when(z == last - 1)
    def _():
        send_weights(last - 1, last)

    def one_layer(layer, carry):
        for g in range(GROUPS):
            mix(layer, g)

        @pl.when(layer < z)
        def _():
            @pl.when(layer + 1 < z)
            def _():
                await_weights(layer + 1)

            spread_gains(layer + 1)
            for pair in range(ctx_size // 2):
                project(layer + 1, pair)

        for g in range(GROUPS):
            sq_wait(sq_send, layer, g)
        return carry

    lax.fori_loop(0, z + 1, one_layer, 0)

    own_out().wait()
    for d in FAR_FIRST:
        tok_copy(d).wait_send()
    for d in FAR_FIRST:
        to = partner(c, d)
        pltpu.make_async_remote_copy(
            stream.at[rows(to)], out_ref.at[0, 0, :, cols(c)],
            out_send.at[to], out_recv.at[to], device_id=(to, z), device_id_type=MESH,
        ).wait()

    @pl.when(z == 0)
    def _():
        weights_sent(0, last - 1)

    @pl.when(z == last - 1)
    def _():
        for to in range(1, last - 1):
            weights_sent(0, to)

    for layer in range(1, last):
        @pl.when(z == layer)
        def _():
            for to in range(layer + 1, sections if layer == last - 1 else last):
                weights_sent(layer, to)


def relay(tokens, w_qkv, norm_gain, out_gain):
    ctx_size, sections = lax.axis_size("ctx"), lax.axis_size("pipe")
    rows, features = tokens.shape[1:]
    all_heads, dim = w_qkv.shape[1:3]
    heads = all_heads // ctx_size
    width = heads * dim
    length = ctx_size * rows
    dma = pltpu.SemaphoreType.DMA
    return pl.pallas_call(
        functools.partial(relay_kernel, (ctx_size, sections, heads, dim, rows)),
        out_shape=pltpu.VMEM((1,) + tokens.shape, jnp.bfloat16),
        in_specs=[pl.BlockSpec(memory_space=pl.ANY)] * 4,
        out_specs=pl.BlockSpec(memory_space=pltpu.VMEM),
        scratch_shapes=[
            pltpu.VMEM((rows, features), jnp.bfloat16),
            pltpu.VMEM((length, width), jnp.bfloat16),
            pltpu.VMEM((heads, ctx_size, dim, rows), jnp.bfloat16),
            pltpu.VMEM((heads, dim, 3 * dim), jnp.bfloat16),
            pltpu.VMEM((1, width), jnp.float32),
            pltpu.VMEM((sections, heads, 2 * dim, dim), jnp.bfloat16),
            pltpu.VMEM((sections, 1, width), jnp.float32),
            pltpu.VMEM((heads, dim, rows), jnp.float32),
            pltpu.VMEM((heads, ctx_size, dim, rows), jnp.float32),
            pltpu.VMEM((heads, ctx_size, rows + dim, rows), jnp.bfloat16),
            pltpu.VMEM((heads, dim, dim), jnp.float32),
            pltpu.VMEM((sections + 1, ctx_size, ctx_size, rows), jnp.float32),
            dma((5,)),
            dma((ctx_size,)),
            dma((ctx_size,)),
            dma((sections, GROUPS)),
            dma((sections, GROUPS)),
            dma((sections, heads + 1)),
            dma((sections, heads + 1)),
            dma((ctx_size,)),
            dma((ctx_size,)),
        ],
        compiler_params=pltpu.CompilerParams(collective_id=0, has_side_effects=True),
    )(tokens, w_qkv, norm_gain, out_gain)


def solution(mesh):
    ctx_size, sections = mesh.shape["ctx"], mesh.shape["pipe"]

    def body(tokens, w_qkv, norm_gain, out_gain):
        micro_count, rows = tokens.shape[:2]
        fits = (
            ctx_size == 8
            and sections == 4
            and micro_count == 1
            and rows == 128
            and w_qkv.shape[1] == 2 * ctx_size
            and w_qkv.shape[2] == 128
        )
        return (relay if fits else shards)(tokens, w_qkv, norm_gain, out_gain)

    placed = (P(None, "ctx", None), P("pipe", None, None, None), P("pipe", None), P("pipe", None))
    return jax.shard_map(
        body, mesh=mesh, in_specs=placed, out_specs=P("pipe", None, "ctx", None), check_vma=False
    )
```

```python
import functools

import jax
import jax.numpy as jnp
from jax import lax
from jax.experimental import pallas as pl
from jax.experimental.pallas import tpu as pltpu
from jax.sharding import PartitionSpec as P

epsilon = 1e-06


def shifted(block, axis, distance):
    devices = range(lax.axis_size(axis))
    route = [(i - distance, i) for i in devices if i - distance in devices]
    return lax.ppermute(block, axis, route)


def run_layer(stream, gain_in, weights, gain_out):
    row_count = stream.shape[0]
    head_count = weights.shape[0]
    head_dim = weights.shape[1]
    widened = stream.astype(jnp.float32)
    normed = (
        widened * lax.rsqrt(jnp.mean(widened * widened, -1, keepdims=True) + epsilon) * gain_in
    ).astype(jnp.bfloat16)
    projected = jnp.einsum(
        "thd,hde->hte",
        normed.reshape(row_count, head_count, head_dim),
        weights,
        preferred_element_type=jnp.float32,
    )
    queries = (projected[..., :head_dim] * head_dim ** (-0.5)).astype(jnp.bfloat16)
    keys_local = projected[..., head_dim : 2 * head_dim].astype(jnp.bfloat16)
    values_local = projected[..., 2 * head_dim :].astype(jnp.bfloat16)
    kv_state = jnp.einsum(
        "hte,htf->hef", keys_local, values_local, preferred_element_type=jnp.float32
    )
    flat_state = kv_state.reshape(1, head_count * head_dim, head_dim)
    spread = lax.all_to_all(
        flat_state.astype(jnp.bfloat16), "ctx", split_axis=1, concat_axis=0, tiled=True
    ).astype(flat_state.dtype)
    running = jnp.cumsum(spread, axis=0)
    lower = jnp.concatenate([jnp.zeros_like(spread[:1]), running[:-1]], axis=0)
    returned = lax.all_to_all(
        lower.astype(jnp.bfloat16), "ctx", split_axis=0, concat_axis=1, tiled=True
    ).astype(lower.dtype)
    prefix = returned.reshape(kv_state.shape)
    scores = jnp.einsum("hte,hse->hts", queries, keys_local, preferred_element_type=jnp.float32)
    positions = jnp.arange(row_count, dtype=jnp.int32)
    causal = positions[:, None] >= positions[None, :]
    masked = jnp.where(causal, scores, 0.0).astype(jnp.bfloat16)
    mixed_heads = jnp.einsum(
        "hts,hsf->htf", masked, values_local, preferred_element_type=jnp.float32
    )
    mixed_heads = mixed_heads + jnp.einsum(
        "hte,hef->htf", queries, prefix.astype(jnp.bfloat16), preferred_element_type=jnp.float32
    )
    mixed_heads = mixed_heads * lax.rsqrt(
        jnp.mean(mixed_heads * mixed_heads, -1, keepdims=True) + epsilon
    )
    branch = jnp.transpose(mixed_heads, (1, 0, 2)).reshape(row_count, head_count * head_dim)
    return (widened + branch * gain_out).astype(jnp.bfloat16)


def shards(tokens, w_qkv, norm_gain, out_gain):
    section_count = lax.axis_size("pipe")
    section_index = lax.axis_index("pipe")
    micro_count = tokens.shape[0]
    hidden_buffer = jnp.zeros(tokens.shape, jnp.bfloat16)
    carried = jnp.zeros(tokens.shape[1:], jnp.bfloat16)
    total_steps = micro_count + section_count - 1
    for tick_index in range(total_steps):
        fresh = tokens[min(tick_index, micro_count - 1)]
        layer_input = jnp.where(section_index == 0, fresh, carried)
        result = run_layer(layer_input, norm_gain[0], w_qkv[0], out_gain[0])
        micro_index = tick_index - section_index
        usable = (micro_index >= 0) & (micro_index < micro_count)
        slot_index = jnp.clip(micro_index, 0, micro_count - 1)
        previous = lax.dynamic_index_in_dim(hidden_buffer, slot_index, 0, keepdims=False)
        hidden_buffer = lax.dynamic_update_index_in_dim(
            hidden_buffer, jnp.where(usable, result, previous), slot_index, 0
        )
        if tick_index + 1 < total_steps:
            carried = shifted(result, "pipe", 1)
    return hidden_buffer[None]


MESH = pl.DeviceIdType.MESH
FAR_FIRST = (6, 7, 2, 4, 3, 5, 1)


def partner(index, flips):
    total = 0
    for bit in (1, 2, 4):
        own = lax.rem(index // bit, 2)
        total = total + (lax.rem(own + 1, 2) if flips & bit else own) * bit
    return total


def lanes_to_rows(row):
    return jnp.broadcast_to(row, (128, row.shape[1])).T


def product(a, b):
    return jnp.dot(a, b, preferred_element_type=jnp.float32)


GROUPS = (4, 2, 2)


def relay_kernel(
    sizes,
    tok_ref,
    w_ref,
    gin_ref,
    gout_ref,
    out_ref,
    own,
    stream,
    turned,
    raw,
    gain_in,
    gain_out,
    folded_maps,
    weights,
    gains,
    gain_cols,
    left,
    right,
    state,
    squares,
    local_sem,
    tok_send,
    tok_recv,
    sq_send,
    sq_recv,
    w_send,
    w_recv,
    out_send,
    out_recv,
):
    ctx_size, sections, dim, tokens = sizes
    features = 2 * ctx_size * dim
    c = lax.axis_index("ctx")
    z = lax.axis_index("pipe")
    side = lax.rem(z, 2)
    base = z - side
    top = base + 1
    other = base + 1 - side
    me = side * ctx_size + c

    def cols(head):
        return pl.ds(pl.multiple_of(head * dim, dim), dim)

    def rows(device):
        return pl.ds(pl.multiple_of(device * tokens, tokens), tokens)

    local = [
        pltpu.make_async_copy(tok_ref.at[0], own, local_sem.at[0]),
        pltpu.make_async_copy(tok_ref.at[0, :, cols(me)], stream.at[0, rows(c)], local_sem.at[1]),
    ]
    parts = []
    for q in range(2):
        head = q * ctx_size + c
        parts += [
            pltpu.make_async_copy(w_ref.at[0, head], raw.at[q], local_sem.at[2 + 3 * q]),
            pltpu.make_async_copy(gin_ref.at[:, cols(head)], gain_in.at[q], local_sem.at[3 + 3 * q]),
            pltpu.make_async_copy(gout_ref.at[:, cols(head)], gain_out.at[q], local_sem.at[4 + 3 * q]),
        ]
    for copy in local + parts:
        copy.start()

    peers = [(d, other) for d in FAR_FIRST + (0,)] + [(d, z) for d in FAR_FIRST]
    barrier = pltpu.get_barrier_semaphore()
    for d, plane in peers:
        pl.semaphore_signal(barrier, 1, device_id=(partner(c, d), plane), device_id_type=MESH)
    for step in range(2):
        away = lax.rem(base + 2 + step, sections)
        pl.semaphore_signal(barrier, 1, device_id=(c, away), device_id_type=MESH)

    def fold():
        for copy in parts:
            copy.wait()
        for q in range(2):
            across = gain_in[q]
            query = raw[q, :, :dim]
            key = raw[q, :, dim : 2 * dim]
            value = raw[q, :, 2 * dim :].astype(jnp.float32)
            crossed = lax.dot_general(
                key, query, (((1,), (1,)), ((), ())), preferred_element_type=jnp.float32
            )
            crossed = crossed * (across * dim ** (-0.5)) * lanes_to_rows(across)
            folded_maps[q, :dim] = crossed.astype(jnp.bfloat16)
            folded_maps[q, dim:] = (value.T * across).astype(jnp.bfloat16)
        weights[z] = folded_maps[side]
        gains[z] = gain_out[side]

    @pl.when(z == 0)
    def _():
        fold()

    local[0].wait()
    folded = jnp.zeros((tokens, 128), jnp.float32)
    for i in range(features // 128):
        piece = own[:, i * 128 : (i + 1) * 128].astype(jnp.float32)
        folded = folded + piece * piece
    total = jnp.sum(folded.T, 0, keepdims=True)
    which = lax.broadcasted_iota(jnp.int32, (ctx_size, tokens), 0)
    squares[0, me] = jnp.where(which == c, jnp.broadcast_to(total, (ctx_size, tokens)), 0.0)
    away = (1 - side) * ctx_size
    squares[0, pl.ds(away, ctx_size)] = jnp.zeros((ctx_size, ctx_size, tokens), jnp.float32)

    pl.semaphore_wait(barrier, len(peers) + 2)

    def tok_copy(d):
        to = partner(c, d)
        return pltpu.make_async_remote_copy(
            tok_ref.at[0, :, cols(side * ctx_size + to)], stream.at[0, rows(c)],
            tok_send.at[d], tok_recv.at[d], device_id=(to, z), device_id_type=MESH,
        )

    def part(g):
        return pl.ds(sum(GROUPS[:g]), GROUPS[g])

    def first_sq_copy(d):
        return pltpu.make_async_remote_copy(
            squares.at[0, me], squares.at[0, me], sq_send.at[0, 0], sq_recv.at[0, 0],
            device_id=(partner(c, d), z), device_id_type=MESH,
        )

    def first_sq_wait(sem):
        every = squares.at[0, pl.ds(0, ctx_size - 1)]
        pltpu.make_async_copy(every, every, sem.at[0, 0]).wait()

    def sq_copy(layer, g, d, plane):
        return pltpu.make_async_remote_copy(
            squares.at[layer, me, part(g)], squares.at[layer, me, part(g)],
            sq_send.at[layer, g], sq_recv.at[layer, g],
            device_id=(partner(c, d), plane), device_id_type=MESH,
        )

    def sq_wait(sem, layer, g):
        every = squares.at[layer, pl.ds(0, len(peers)), part(g)]
        pltpu.make_async_copy(every, every, sem.at[layer, g]).wait()

    def w_pieces(layer, q):
        return [
            (folded_maps.at[q, pl.ds(0, dim)], weights.at[layer, pl.ds(0, dim)]),
            (folded_maps.at[q, pl.ds(dim, dim)], weights.at[layer, pl.ds(dim, dim)]),
            (gain_out.at[q], gains.at[layer]),
        ]

    def w_copy(layer, to, i):
        source, target = w_pieces(layer, to % 2)[i]
        return pltpu.make_async_remote_copy(
            source, target, w_send.at[to, i], w_recv.at[layer, i],
            device_id=(c, to), device_id_type=MESH,
        )

    def send_weights(layer, *targets):
        for i in range(3):
            for to in targets:
                w_copy(layer, to, i).start()

    def weights_sent(layer, *targets):
        for to in targets:
            for i in range(3):
                w_copy(layer, to, i).wait_send()

    def await_piece(layer, i):
        source, target = w_pieces(layer, 0)[i]
        pltpu.make_async_remote_copy(
            source, target, w_send.at[0, i], w_recv.at[layer, i],
            device_id=(c, other), device_id_type=MESH,
        ).wait_recv()

    @pl.when(z == 0)
    def _():
        send_weights(0, 3, 2)

    for d in FAR_FIRST:
        tok_copy(d).start()
    for d in FAR_FIRST:
        first_sq_copy(d).start()

    @pl.when(z > 0)
    def _():
        fold()

    at_row = lax.broadcasted_iota(jnp.int32, (tokens, tokens), 0)
    at_col = lax.broadcasted_iota(jnp.int32, (tokens, tokens), 1)
    causal = at_row <= at_col

    def out_copy(slot, plane, block):
        return pltpu.make_async_remote_copy(
            stream.at[slot, rows(block)], out_ref.at[0, 0, :, cols(me)],
            out_send.at[slot, block], out_recv.at[me],
            device_id=(block, plane), device_id_type=MESH,
        )

    def own_out(slot):
        return pltpu.make_async_copy(
            stream.at[slot, rows(c)], out_ref.at[0, 0, :, cols(me)], local_sem.at[0]
        )

    def each_out(slot, plane, blocks, remote, here):
        for block in blocks:
            mine = jnp.logical_and(c == block, z == plane)

            @pl.when(jnp.logical_not(mine))
            def _():
                remote(out_copy(slot, plane, block))

            @pl.when(mine)
            def _():
                here(own_out(slot))

    def attend(slot, block, queries):
        queries = queries.astype(jnp.bfloat16)
        right[block, tokens:] = queries
        scores = product(stream[slot, rows(block)], queries)
        right[block, :tokens] = jnp.where(causal, scores, 0.0).astype(jnp.bfloat16)

    def pair_of(pair):
        return jnp.concatenate([turned[2 * pair], turned[2 * pair + 1]], 1)

    def project(layer, slot, pair):
        projected = product(weights[layer], pair_of(pair))
        for i in range(2):
            here = projected[:, i * tokens : (i + 1) * tokens]
            left[2 * pair + i] = here[dim:]
            attend(slot, 2 * pair + i, here[:dim])

    def turn(block):
        turned[block] = stream[0, rows(block)].T

    def attend_first(block):
        attend(0, block, product(weights[0, :dim], turned[block]))

    def spread_gains(layer):
        gain_cols[...] = lanes_to_rows(gains[layer])

    def mix(layer, g):
        first = sum(GROUPS[:g])
        span = GROUPS[g]
        slot = lax.rem(layer, 2)

        @pl.when(layer > 0)
        def _():
            sq_wait(sq_recv, layer, g)

        mean = jnp.sum(squares[layer, :, first : first + span], 0) * (1.0 / features)
        scale = lax.rsqrt(mean + epsilon)
        twice = scale * scale
        sums = []
        running = state[...] if g else jnp.zeros((dim, dim), jnp.float32)
        for i in range(span):
            block = first + i
            own_scale, own_twice = scale[i : i + 1], twice[i : i + 1]
            scaled = (left[block] * own_twice).astype(jnp.bfloat16)
            mixed = product(
                jnp.concatenate([scaled, running.astype(jnp.bfloat16)], 1), right[block]
            )
            if block + 1 < ctx_size:
                running = running + product(scaled, stream[slot, rows(block)])
            power = jnp.sum(mixed * mixed, 0, keepdims=True) * (1.0 / dim)
            factor = own_scale * lax.rsqrt(own_twice * power + epsilon)
            leaving = turned[block].astype(jnp.float32) + gain_cols[...] * (mixed * factor)
            rounded = leaving.astype(jnp.bfloat16)
            turned[block] = rounded
            stream[1 - slot, rows(block)] = rounded.T
            sums.append(jnp.sum(leaving * leaving, 0, keepdims=True))
        if g + 1 < len(GROUPS):
            state[...] = running
        squares[layer + 1, me, first : first + span] = jnp.concatenate(sums, 0)

        @pl.when(layer < top)
        def _():
            for d, plane in peers:
                sq_copy(layer + 1, g, d, plane).start()

        @pl.when(layer == top)
        def _():
            each_out(
                0, top, range(first, first + span), lambda copy: copy.start(), lambda copy: copy.start()
            )

        if g + 1 == len(GROUPS):
            @pl.when(layer == base)
            def _():
                each_out(
                    1, base, range(ctx_size), lambda copy: copy.start(), lambda copy: copy.start()
                )

    @pl.when(z == 1)
    def _():
        for d in (6, 7):
            tok_copy(d).wait_recv()
        send_weights(1, 3, 2)

    @pl.when(z == 0)
    def _():
        weights_sent(0, 3, 2)
        send_weights(0, 1)

    def await_first(i):
        @pl.when(z > 0)
        def _():
            await_piece(0, i)

    def arrive(pair):
        if pair == (6, 7):
            @pl.when(z != 1)
            def _():
                for d in pair:
                    tok_copy(d).wait_recv()
        else:
            for d in pair:
                tok_copy(d).wait_recv()
        for d in pair:
            turn(partner(c, d))

    local[1].wait()
    turn(c)
    arrive((1,))
    arrive((6, 7))
    await_first(0)
    for d in (0, 1, 6, 7):
        attend_first(partner(c, d))
    for pair in ((2, 4), (3, 5)):
        arrive(pair)
        for d in pair:
            attend_first(partner(c, d))
    await_first(1)
    for pair in range(ctx_size // 2):
        values = product(weights[0, dim:], pair_of(pair))
        for i in range(2):
            left[2 * pair + i] = values[:, i * tokens : (i + 1) * tokens]
    await_first(2)
    spread_gains(0)

    for layer, to in ((1, 0), (2, 3), (3, 2)):
        @pl.when(z == layer)
        def _():
            send_weights(layer, to)

    first_sq_wait(sq_recv)

    def one_layer(layer, carry):
        for g in range(len(GROUPS)):
            mix(layer, g)

        @pl.when(layer < top)
        def _():
            @pl.when(layer + 1 != z)
            def _():
                for i in range(3):
                    await_piece(layer + 1, i)

            spread_gains(layer + 1)
            for pair in range(ctx_size // 2):
                project(layer + 1, lax.rem(layer + 1, 2), pair)

        @pl.when(layer > 0)
        def _():
            for g in range(len(GROUPS)):
                sq_wait(sq_send, layer, g)

        return carry

    lax.fori_loop(0, base + 2, one_layer, 0)

    first_sq_wait(sq_send)
    for d in FAR_FIRST:
        tok_copy(d).wait_send()
    for layer, targets in ((0, (1,)), (1, (3, 2, 0)), (2, (3,)), (3, (2,))):
        @pl.when(z == layer)
        def _():
            weights_sent(layer, *targets)

    each_out(1, base, range(ctx_size), lambda copy: copy.wait_send(), lambda copy: copy.wait())
    each_out(0, top, range(ctx_size), lambda copy: copy.wait_send(), lambda copy: copy.wait())
    for d, plane in peers:
        source = partner(c, d)
        head = source + lax.rem(plane, 2) * ctx_size
        pltpu.make_async_remote_copy(
            stream.at[0, rows(source)], out_ref.at[0, 0, :, cols(head)],
            out_send.at[0, source], out_recv.at[head],
            device_id=(source, plane), device_id_type=MESH,
        ).wait_recv()


def relay(tokens, w_qkv, norm_gain, out_gain):
    ctx_size, sections = lax.axis_size("ctx"), lax.axis_size("pipe")
    rows, features = tokens.shape[1:]
    dim = w_qkv.shape[2]
    length = ctx_size * rows
    dma = pltpu.SemaphoreType.DMA
    return pl.pallas_call(
        functools.partial(relay_kernel, (ctx_size, sections, dim, rows)),
        out_shape=pltpu.VMEM((1,) + tokens.shape, jnp.bfloat16),
        in_specs=[pl.BlockSpec(memory_space=pl.ANY)] * 4,
        out_specs=pl.BlockSpec(memory_space=pltpu.VMEM),
        scratch_shapes=[
            pltpu.VMEM((rows, features), jnp.bfloat16),
            pltpu.VMEM((2, length, dim), jnp.bfloat16),
            pltpu.VMEM((ctx_size, dim, rows), jnp.bfloat16),
            pltpu.VMEM((2, dim, 3 * dim), jnp.bfloat16),
            pltpu.VMEM((2, 1, dim), jnp.float32),
            pltpu.VMEM((2, 1, dim), jnp.float32),
            pltpu.VMEM((2, 2 * dim, dim), jnp.bfloat16),
            pltpu.VMEM((sections, 2 * dim, dim), jnp.bfloat16),
            pltpu.VMEM((sections, 1, dim), jnp.float32),
            pltpu.VMEM((dim, rows), jnp.float32),
            pltpu.VMEM((ctx_size, dim, rows), jnp.float32),
            pltpu.VMEM((ctx_size, rows + dim, rows), jnp.bfloat16),
            pltpu.VMEM((dim, dim), jnp.float32),
            pltpu.VMEM((sections + 1, 2 * ctx_size, ctx_size, rows), jnp.float32),
            dma((8,)),
            dma((ctx_size,)),
            dma((ctx_size,)),
            dma((sections, len(GROUPS))),
            dma((sections, len(GROUPS))),
            dma((sections, 3)),
            dma((sections, 3)),
            dma((2, ctx_size)),
            dma((2 * ctx_size,)),
        ],
        compiler_params=pltpu.CompilerParams(collective_id=0, has_side_effects=True),
    )(tokens, w_qkv, norm_gain, out_gain)


def solution(mesh):
    ctx_size, sections = mesh.shape["ctx"], mesh.shape["pipe"]

    def body(tokens, w_qkv, norm_gain, out_gain):
        micro_count, rows = tokens.shape[:2]
        fits = (
            ctx_size == 8
            and sections == 4
            and micro_count == 1
            and rows == 128
            and w_qkv.shape[1] == 2 * ctx_size
            and w_qkv.shape[2] == 128
        )
        return (relay if fits else shards)(tokens, w_qkv, norm_gain, out_gain)

    placed = (P(None, "ctx", None), P("pipe", None, None, None), P("pipe", None), P("pipe", None))
    return jax.shard_map(
        body, mesh=mesh, in_specs=placed, out_specs=P("pipe", None, "ctx", None), check_vma=False
    )
```

```python
import functools

import jax
import jax.numpy as jnp
from jax import lax
from jax.experimental import pallas as pl
from jax.experimental.pallas import tpu as pltpu
from jax.sharding import PartitionSpec as P

epsilon = 1e-06


def shifted(block, axis, distance):
    devices = range(lax.axis_size(axis))
    route = [(i - distance, i) for i in devices if i - distance in devices]
    return lax.ppermute(block, axis, route)


def run_layer(stream, gain_in, weights, gain_out):
    row_count = stream.shape[0]
    head_count = weights.shape[0]
    head_dim = weights.shape[1]
    widened = stream.astype(jnp.float32)
    normed = (
        widened * lax.rsqrt(jnp.mean(widened * widened, -1, keepdims=True) + epsilon) * gain_in
    ).astype(jnp.bfloat16)
    projected = jnp.einsum(
        "thd,hde->hte",
        normed.reshape(row_count, head_count, head_dim),
        weights,
        preferred_element_type=jnp.float32,
    )
    queries = (projected[..., :head_dim] * head_dim ** (-0.5)).astype(jnp.bfloat16)
    keys_local = projected[..., head_dim : 2 * head_dim].astype(jnp.bfloat16)
    values_local = projected[..., 2 * head_dim :].astype(jnp.bfloat16)
    kv_state = jnp.einsum(
        "hte,htf->hef", keys_local, values_local, preferred_element_type=jnp.float32
    )
    flat_state = kv_state.reshape(1, head_count * head_dim, head_dim)
    spread = lax.all_to_all(
        flat_state.astype(jnp.bfloat16), "ctx", split_axis=1, concat_axis=0, tiled=True
    ).astype(flat_state.dtype)
    running = jnp.cumsum(spread, axis=0)
    lower = jnp.concatenate([jnp.zeros_like(spread[:1]), running[:-1]], axis=0)
    returned = lax.all_to_all(
        lower.astype(jnp.bfloat16), "ctx", split_axis=0, concat_axis=1, tiled=True
    ).astype(lower.dtype)
    prefix = returned.reshape(kv_state.shape)
    scores = jnp.einsum("hte,hse->hts", queries, keys_local, preferred_element_type=jnp.float32)
    positions = jnp.arange(row_count, dtype=jnp.int32)
    causal = positions[:, None] >= positions[None, :]
    masked = jnp.where(causal, scores, 0.0).astype(jnp.bfloat16)
    mixed_heads = jnp.einsum(
        "hts,hsf->htf", masked, values_local, preferred_element_type=jnp.float32
    )
    mixed_heads = mixed_heads + jnp.einsum(
        "hte,hef->htf", queries, prefix.astype(jnp.bfloat16), preferred_element_type=jnp.float32
    )
    mixed_heads = mixed_heads * lax.rsqrt(
        jnp.mean(mixed_heads * mixed_heads, -1, keepdims=True) + epsilon
    )
    branch = jnp.transpose(mixed_heads, (1, 0, 2)).reshape(row_count, head_count * head_dim)
    return (widened + branch * gain_out).astype(jnp.bfloat16)


def shards(tokens, w_qkv, norm_gain, out_gain):
    section_count = lax.axis_size("pipe")
    section_index = lax.axis_index("pipe")
    micro_count = tokens.shape[0]
    hidden_buffer = jnp.zeros(tokens.shape, jnp.bfloat16)
    carried = jnp.zeros(tokens.shape[1:], jnp.bfloat16)
    total_steps = micro_count + section_count - 1
    for tick_index in range(total_steps):
        fresh = tokens[min(tick_index, micro_count - 1)]
        layer_input = jnp.where(section_index == 0, fresh, carried)
        result = run_layer(layer_input, norm_gain[0], w_qkv[0], out_gain[0])
        micro_index = tick_index - section_index
        usable = (micro_index >= 0) & (micro_index < micro_count)
        slot_index = jnp.clip(micro_index, 0, micro_count - 1)
        previous = lax.dynamic_index_in_dim(hidden_buffer, slot_index, 0, keepdims=False)
        hidden_buffer = lax.dynamic_update_index_in_dim(
            hidden_buffer, jnp.where(usable, result, previous), slot_index, 0
        )
        if tick_index + 1 < total_steps:
            carried = shifted(result, "pipe", 1)
    return hidden_buffer[None]


MESH = pl.DeviceIdType.MESH
FAR_FIRST = (6, 7, 2, 4, 3, 5, 1)


def partner(index, flips):
    total = 0
    for bit in (1, 2, 4):
        own = lax.rem(index // bit, 2)
        total = total + (lax.rem(own + 1, 2) if flips & bit else own) * bit
    return total


def lanes_to_rows(row):
    return jnp.broadcast_to(row, (128, row.shape[1])).T


def product(a, b):
    return jnp.dot(a, b, preferred_element_type=jnp.float32)


GROUPS = (3, 3, 2)


def relay_kernel(
    sizes,
    tok_ref,
    w_ref,
    gin_ref,
    gout_ref,
    out_ref,
    own,
    stream,
    turned,
    raw,
    gain_in,
    gain_out,
    folded_maps,
    weights,
    gains,
    gain_cols,
    left,
    right,
    state,
    squares,
    local_sem,
    tok_send,
    tok_recv,
    sq_send,
    sq_recv,
    w_send,
    w_recv,
    out_send,
    out_recv,
):
    ctx_size, sections, dim, tokens = sizes
    features = 2 * ctx_size * dim
    c = lax.axis_index("ctx")
    z = lax.axis_index("pipe")
    side = lax.rem(z, 2)
    base = z - side
    top = base + 1
    other = base + 1 - side
    me = side * ctx_size + c

    def cols(head):
        return pl.ds(pl.multiple_of(head * dim, dim), dim)

    def rows(device):
        return pl.ds(pl.multiple_of(device * tokens, tokens), tokens)

    local = [
        pltpu.make_async_copy(tok_ref.at[0], own, local_sem.at[0]),
        pltpu.make_async_copy(tok_ref.at[0, :, cols(me)], stream.at[0, rows(c)], local_sem.at[1]),
    ]
    parts = []
    for q in range(2):
        head = q * ctx_size + c
        parts += [
            pltpu.make_async_copy(w_ref.at[0, head], raw.at[q], local_sem.at[2 + 3 * q]),
            pltpu.make_async_copy(gin_ref.at[:, cols(head)], gain_in.at[q], local_sem.at[3 + 3 * q]),
            pltpu.make_async_copy(gout_ref.at[:, cols(head)], gain_out.at[q], local_sem.at[4 + 3 * q]),
        ]
    for copy in local + parts:
        copy.start()

    peers = [(d, plane) for plane in (other, z) for d in (6, 7)]
    peers += [(d, plane) for plane in (other, z) for d in (2, 4, 3, 5)]
    peers += [(0, other), (1, other), (1, z)]
    barrier = pltpu.get_barrier_semaphore()
    for d, plane in peers:
        pl.semaphore_signal(barrier, 1, device_id=(partner(c, d), plane), device_id_type=MESH)
    for step in range(2):
        away = lax.rem(base + 2 + step, sections)
        pl.semaphore_signal(barrier, 1, device_id=(c, away), device_id_type=MESH)

    def fold():
        for copy in parts:
            copy.wait()
        for q in range(2):
            across = gain_in[q]
            query = raw[q, :, :dim]
            key = raw[q, :, dim : 2 * dim]
            value = raw[q, :, 2 * dim :].astype(jnp.float32)
            crossed = lax.dot_general(
                key, query, (((1,), (1,)), ((), ())), preferred_element_type=jnp.float32
            )
            crossed = crossed * (across * dim ** (-0.5)) * lanes_to_rows(across)
            folded_maps[q, :dim] = crossed.astype(jnp.bfloat16)
            folded_maps[q, dim:] = (value.T * across).astype(jnp.bfloat16)
        weights[z] = folded_maps[side]
        gains[z] = gain_out[side]

    @pl.when(z == 0)
    def _():
        fold()

    local[0].wait()
    folded = jnp.zeros((tokens, 128), jnp.float32)
    for i in range(features // 128):
        piece = own[:, i * 128 : (i + 1) * 128].astype(jnp.float32)
        folded = folded + piece * piece
    total = jnp.sum(folded.T, 0, keepdims=True)
    which = lax.broadcasted_iota(jnp.int32, (ctx_size, tokens), 0)
    squares[0, me] = jnp.where(which == c, jnp.broadcast_to(total, (ctx_size, tokens)), 0.0)
    away = (1 - side) * ctx_size
    squares[0, pl.ds(away, ctx_size)] = jnp.zeros((ctx_size, ctx_size, tokens), jnp.float32)

    pl.semaphore_wait(barrier, len(peers) + 2)

    def tok_copy(d):
        to = partner(c, d)
        return pltpu.make_async_remote_copy(
            tok_ref.at[0, :, cols(side * ctx_size + to)], stream.at[0, rows(c)],
            tok_send.at[d], tok_recv.at[d], device_id=(to, z), device_id_type=MESH,
        )

    def part(g):
        return pl.ds(sum(GROUPS[:g]), GROUPS[g])

    def first_sq_copy(d):
        return pltpu.make_async_remote_copy(
            squares.at[0, me], squares.at[0, me], sq_send.at[0, 0], sq_recv.at[0, 0],
            device_id=(partner(c, d), z), device_id_type=MESH,
        )

    def first_sq_wait(sem):
        every = squares.at[0, pl.ds(0, ctx_size - 1)]
        pltpu.make_async_copy(every, every, sem.at[0, 0]).wait()

    def sq_copy(layer, g, d, plane):
        return pltpu.make_async_remote_copy(
            squares.at[layer, me, part(g)], squares.at[layer, me, part(g)],
            sq_send.at[layer, g], sq_recv.at[layer, g],
            device_id=(partner(c, d), plane), device_id_type=MESH,
        )

    def sq_wait(sem, layer, g):
        every = squares.at[layer, pl.ds(0, len(peers)), part(g)]
        pltpu.make_async_copy(every, every, sem.at[layer, g]).wait()

    def w_pieces(layer, q):
        return [
            (folded_maps.at[q, pl.ds(0, dim)], weights.at[layer, pl.ds(0, dim)]),
            (folded_maps.at[q, pl.ds(dim, dim)], weights.at[layer, pl.ds(dim, dim)]),
            (gain_out.at[q], gains.at[layer]),
        ]

    def w_copy(layer, to, i):
        source, target = w_pieces(layer, to % 2)[i]
        return pltpu.make_async_remote_copy(
            source, target, w_send.at[to, i], w_recv.at[layer, i],
            device_id=(c, to), device_id_type=MESH,
        )

    def send_weights(layer, *targets):
        for i in range(3):
            for to in targets:
                w_copy(layer, to, i).start()

    def weights_sent(layer, *targets):
        for to in targets:
            for i in range(3):
                w_copy(layer, to, i).wait_send()

    def await_piece(layer, i):
        source, target = w_pieces(layer, 0)[i]
        pltpu.make_async_remote_copy(
            source, target, w_send.at[0, i], w_recv.at[layer, i],
            device_id=(c, other), device_id_type=MESH,
        ).wait_recv()

    @pl.when(z == 0)
    def _():
        send_weights(0, 3, 2)

    for d in FAR_FIRST:
        tok_copy(d).start()
    for d in FAR_FIRST:
        first_sq_copy(d).start()

    @pl.when(z > 0)
    def _():
        fold()

    for layer, to in ((1, 0), (2, 3), (3, 2)):
        @pl.when(z == layer)
        def _():
            send_weights(layer, to)

    at_row = lax.broadcasted_iota(jnp.int32, (tokens, tokens), 0)
    at_col = lax.broadcasted_iota(jnp.int32, (tokens, tokens), 1)
    causal = at_row <= at_col

    def out_copy(slot, plane, block):
        return pltpu.make_async_remote_copy(
            stream.at[slot, rows(block)], out_ref.at[0, 0, :, cols(me)],
            out_send.at[slot, block], out_recv.at[me],
            device_id=(block, plane), device_id_type=MESH,
        )

    def own_out(slot):
        return pltpu.make_async_copy(
            stream.at[slot, rows(c)], out_ref.at[0, 0, :, cols(me)], local_sem.at[0]
        )

    def each_out(slot, plane, blocks, remote, here):
        for block in blocks:
            mine = jnp.logical_and(c == block, z == plane)

            @pl.when(jnp.logical_not(mine))
            def _():
                remote(out_copy(slot, plane, block))

            @pl.when(mine)
            def _():
                here(own_out(slot))

    def attend(slot, block, queries):
        queries = queries.astype(jnp.bfloat16)
        right[block, tokens:] = queries
        scores = product(stream[slot, rows(block)], queries)
        right[block, :tokens] = jnp.where(causal, scores, 0.0).astype(jnp.bfloat16)

    def pair_of(pair):
        return jnp.concatenate([turned[2 * pair], turned[2 * pair + 1]], 1)

    def project(layer, slot, pair):
        projected = product(weights[layer], pair_of(pair))
        for i in range(2):
            here = projected[:, i * tokens : (i + 1) * tokens]
            left[2 * pair + i] = here[dim:]
            attend(slot, 2 * pair + i, here[:dim])

    def turn(block):
        turned[block] = stream[0, rows(block)].T

    def attend_first(block):
        attend(0, block, product(weights[0, :dim], turned[block]))

    def spread_gains(layer):
        gain_cols[...] = lanes_to_rows(gains[layer])

    def mix(layer, g):
        first = sum(GROUPS[:g])
        span = GROUPS[g]
        slot = lax.rem(layer, 2)

        @pl.when(layer > 0)
        def _():
            sq_wait(sq_recv, layer, g)

        mean = jnp.sum(squares[layer, :, first : first + span], 0) * (1.0 / features)
        scale = lax.rsqrt(mean + epsilon)
        twice = scale * scale
        sums = []
        running = state[...] if g else jnp.zeros((dim, dim), jnp.float32)
        for i in range(span):
            block = first + i
            own_scale, own_twice = scale[i : i + 1], twice[i : i + 1]
            scaled = (left[block] * own_twice).astype(jnp.bfloat16)
            mixed = product(
                jnp.concatenate([scaled, running.astype(jnp.bfloat16)], 1), right[block]
            )
            if block + 1 < ctx_size:
                running = running + product(scaled, stream[slot, rows(block)])
            power = jnp.sum(mixed * mixed, 0, keepdims=True) * (1.0 / dim)
            factor = own_scale * lax.rsqrt(own_twice * power + epsilon)
            leaving = turned[block].astype(jnp.float32) + gain_cols[...] * (mixed * factor)
            rounded = leaving.astype(jnp.bfloat16)
            turned[block] = rounded
            stream[1 - slot, rows(block)] = rounded.T
            sums.append(jnp.sum(leaving * leaving, 0, keepdims=True))
        if g + 1 < len(GROUPS):
            state[...] = running
        squares[layer + 1, me, first : first + span] = jnp.concatenate(sums, 0)

        @pl.when(layer < top)
        def _():
            for d, plane in peers:
                sq_copy(layer + 1, g, d, plane).start()

        @pl.when(layer == top)
        def _():
            each_out(
                0, top, range(first, first + span), lambda copy: copy.start(), lambda copy: copy.start()
            )

        if g + 1 == len(GROUPS):
            @pl.when(layer == base)
            def _():
                each_out(
                    1, base, range(ctx_size), lambda copy: copy.start(), lambda copy: copy.start()
                )

    @pl.when(z == 1)
    def _():
        for d in (6, 7):
            tok_copy(d).wait_recv()
        send_weights(1, 3, 2)

    @pl.when(z == 0)
    def _():
        weights_sent(0, 3, 2)
        send_weights(0, 1)

    def await_first(i):
        @pl.when(z > 0)
        def _():
            await_piece(0, i)

    def arrive(pair):
        if pair == (6, 7):
            @pl.when(z != 1)
            def _():
                for d in pair:
                    tok_copy(d).wait_recv()
        else:
            for d in pair:
                tok_copy(d).wait_recv()
        for d in pair:
            turn(partner(c, d))

    local[1].wait()
    turn(c)
    arrive((1,))
    arrive((6, 7))
    await_first(0)
    for d in (0, 1, 6, 7):
        attend_first(partner(c, d))
    for pair in ((2, 4), (3, 5)):
        arrive(pair)
        for d in pair:
            attend_first(partner(c, d))
    await_first(1)
    for pair in range(ctx_size // 2):
        values = product(weights[0, dim:], pair_of(pair))
        for i in range(2):
            left[2 * pair + i] = values[:, i * tokens : (i + 1) * tokens]
    await_first(2)
    spread_gains(0)

    first_sq_wait(sq_recv)

    def one_layer(layer, carry):
        for g in range(len(GROUPS)):
            mix(layer, g)

        @pl.when(layer < top)
        def _():
            @pl.when(layer + 1 != z)
            def _():
                for i in range(3):
                    await_piece(layer + 1, i)

            spread_gains(layer + 1)
            for pair in range(ctx_size // 2):
                project(layer + 1, lax.rem(layer + 1, 2), pair)

        @pl.when(layer > 0)
        def _():
            for g in range(len(GROUPS)):
                sq_wait(sq_send, layer, g)

        return carry

    lax.fori_loop(0, base + 2, one_layer, 0)

    first_sq_wait(sq_send)
    for d in FAR_FIRST:
        tok_copy(d).wait_send()
    for layer, targets in ((0, (1,)), (1, (3, 2, 0)), (2, (3,)), (3, (2,))):
        @pl.when(z == layer)
        def _():
            weights_sent(layer, *targets)

    each_out(1, base, range(ctx_size), lambda copy: copy.wait_send(), lambda copy: copy.wait())
    each_out(0, top, range(ctx_size), lambda copy: copy.wait_send(), lambda copy: copy.wait())
    for d, plane in peers:
        source = partner(c, d)
        head = source + lax.rem(plane, 2) * ctx_size
        pltpu.make_async_remote_copy(
            stream.at[0, rows(source)], out_ref.at[0, 0, :, cols(head)],
            out_send.at[0, source], out_recv.at[head],
            device_id=(source, plane), device_id_type=MESH,
        ).wait_recv()


def relay(tokens, w_qkv, norm_gain, out_gain):
    ctx_size, sections = lax.axis_size("ctx"), lax.axis_size("pipe")
    rows, features = tokens.shape[1:]
    dim = w_qkv.shape[2]
    length = ctx_size * rows
    dma = pltpu.SemaphoreType.DMA
    return pl.pallas_call(
        functools.partial(relay_kernel, (ctx_size, sections, dim, rows)),
        out_shape=pltpu.VMEM((1,) + tokens.shape, jnp.bfloat16),
        in_specs=[pl.BlockSpec(memory_space=pl.ANY)] * 4,
        out_specs=pl.BlockSpec(memory_space=pltpu.VMEM),
        scratch_shapes=[
            pltpu.VMEM((rows, features), jnp.bfloat16),
            pltpu.VMEM((2, length, dim), jnp.bfloat16),
            pltpu.VMEM((ctx_size, dim, rows), jnp.bfloat16),
            pltpu.VMEM((2, dim, 3 * dim), jnp.bfloat16),
            pltpu.VMEM((2, 1, dim), jnp.float32),
            pltpu.VMEM((2, 1, dim), jnp.float32),
            pltpu.VMEM((2, 2 * dim, dim), jnp.bfloat16),
            pltpu.VMEM((sections, 2 * dim, dim), jnp.bfloat16),
            pltpu.VMEM((sections, 1, dim), jnp.float32),
            pltpu.VMEM((dim, rows), jnp.float32),
            pltpu.VMEM((ctx_size, dim, rows), jnp.float32),
            pltpu.VMEM((ctx_size, rows + dim, rows), jnp.bfloat16),
            pltpu.VMEM((dim, dim), jnp.float32),
            pltpu.VMEM((sections + 1, 2 * ctx_size, ctx_size, rows), jnp.float32),
            dma((8,)),
            dma((ctx_size,)),
            dma((ctx_size,)),
            dma((sections, len(GROUPS))),
            dma((sections, len(GROUPS))),
            dma((sections, 3)),
            dma((sections, 3)),
            dma((2, ctx_size)),
            dma((2 * ctx_size,)),
        ],
        compiler_params=pltpu.CompilerParams(collective_id=0, has_side_effects=True),
    )(tokens, w_qkv, norm_gain, out_gain)


def solution(mesh):
    ctx_size, sections = mesh.shape["ctx"], mesh.shape["pipe"]

    def body(tokens, w_qkv, norm_gain, out_gain):
        micro_count, rows = tokens.shape[:2]
        fits = (
            ctx_size == 8
            and sections == 4
            and micro_count == 1
            and rows == 128
            and w_qkv.shape[1] == 2 * ctx_size
            and w_qkv.shape[2] == 128
        )
        return (relay if fits else shards)(tokens, w_qkv, norm_gain, out_gain)

    placed = (P(None, "ctx", None), P("pipe", None, None, None), P("pipe", None), P("pipe", None))
    return jax.shard_map(
        body, mesh=mesh, in_specs=placed, out_specs=P("pipe", None, "ctx", None), check_vma=False
    )
```

```python
import functools

import jax
import jax.numpy as jnp
from jax import lax
from jax.experimental import pallas as pl
from jax.experimental.pallas import tpu as pltpu
from jax.sharding import PartitionSpec as P

epsilon = 1e-06


def shifted(block, axis, distance):
    devices = range(lax.axis_size(axis))
    route = [(i - distance, i) for i in devices if i - distance in devices]
    return lax.ppermute(block, axis, route)


def run_layer(stream, gain_in, weights, gain_out):
    row_count = stream.shape[0]
    head_count = weights.shape[0]
    head_dim = weights.shape[1]
    widened = stream.astype(jnp.float32)
    normed = (
        widened * lax.rsqrt(jnp.mean(widened * widened, -1, keepdims=True) + epsilon) * gain_in
    ).astype(jnp.bfloat16)
    projected = jnp.einsum(
        "thd,hde->hte",
        normed.reshape(row_count, head_count, head_dim),
        weights,
        preferred_element_type=jnp.float32,
    )
    queries = (projected[..., :head_dim] * head_dim ** (-0.5)).astype(jnp.bfloat16)
    keys_local = projected[..., head_dim : 2 * head_dim].astype(jnp.bfloat16)
    values_local = projected[..., 2 * head_dim :].astype(jnp.bfloat16)
    kv_state = jnp.einsum(
        "hte,htf->hef", keys_local, values_local, preferred_element_type=jnp.float32
    )
    flat_state = kv_state.reshape(1, head_count * head_dim, head_dim)
    spread = lax.all_to_all(
        flat_state.astype(jnp.bfloat16), "ctx", split_axis=1, concat_axis=0, tiled=True
    ).astype(flat_state.dtype)
    running = jnp.cumsum(spread, axis=0)
    lower = jnp.concatenate([jnp.zeros_like(spread[:1]), running[:-1]], axis=0)
    returned = lax.all_to_all(
        lower.astype(jnp.bfloat16), "ctx", split_axis=0, concat_axis=1, tiled=True
    ).astype(lower.dtype)
    prefix = returned.reshape(kv_state.shape)
    scores = jnp.einsum("hte,hse->hts", queries, keys_local, preferred_element_type=jnp.float32)
    positions = jnp.arange(row_count, dtype=jnp.int32)
    causal = positions[:, None] >= positions[None, :]
    masked = jnp.where(causal, scores, 0.0).astype(jnp.bfloat16)
    mixed_heads = jnp.einsum(
        "hts,hsf->htf", masked, values_local, preferred_element_type=jnp.float32
    )
    mixed_heads = mixed_heads + jnp.einsum(
        "hte,hef->htf", queries, prefix.astype(jnp.bfloat16), preferred_element_type=jnp.float32
    )
    mixed_heads = mixed_heads * lax.rsqrt(
        jnp.mean(mixed_heads * mixed_heads, -1, keepdims=True) + epsilon
    )
    branch = jnp.transpose(mixed_heads, (1, 0, 2)).reshape(row_count, head_count * head_dim)
    return (widened + branch * gain_out).astype(jnp.bfloat16)


def shards(tokens, w_qkv, norm_gain, out_gain):
    section_count = lax.axis_size("pipe")
    section_index = lax.axis_index("pipe")
    micro_count = tokens.shape[0]
    hidden_buffer = jnp.zeros(tokens.shape, jnp.bfloat16)
    carried = jnp.zeros(tokens.shape[1:], jnp.bfloat16)
    total_steps = micro_count + section_count - 1
    for tick_index in range(total_steps):
        fresh = tokens[min(tick_index, micro_count - 1)]
        layer_input = jnp.where(section_index == 0, fresh, carried)
        result = run_layer(layer_input, norm_gain[0], w_qkv[0], out_gain[0])
        micro_index = tick_index - section_index
        usable = (micro_index >= 0) & (micro_index < micro_count)
        slot_index = jnp.clip(micro_index, 0, micro_count - 1)
        previous = lax.dynamic_index_in_dim(hidden_buffer, slot_index, 0, keepdims=False)
        hidden_buffer = lax.dynamic_update_index_in_dim(
            hidden_buffer, jnp.where(usable, result, previous), slot_index, 0
        )
        if tick_index + 1 < total_steps:
            carried = shifted(result, "pipe", 1)
    return hidden_buffer[None]


MESH = pl.DeviceIdType.MESH
FAR_FIRST = (6, 7, 2, 4, 3, 5, 1)


def partner(index, flips):
    total = 0
    for bit in (1, 2, 4):
        own = lax.rem(index // bit, 2)
        total = total + (lax.rem(own + 1, 2) if flips & bit else own) * bit
    return total


def lanes_to_rows(row):
    return jnp.broadcast_to(row, (128, row.shape[1])).T


def product(a, b):
    return jnp.dot(a, b, preferred_element_type=jnp.float32)


GROUPS = (3, 3, 2)


def relay_kernel(
    sizes,
    tok_ref,
    w_ref,
    gin_ref,
    gout_ref,
    out_ref,
    own,
    stream,
    turned,
    raw,
    gain_in,
    gain_out,
    folded_maps,
    weights,
    gains,
    gain_cols,
    left,
    right,
    state,
    squares,
    ready_sem,
    local_sem,
    tok_send,
    tok_recv,
    sq_send,
    sq_recv,
    w_send,
    w_recv,
    out_send,
    out_recv,
):
    ctx_size, sections, dim, tokens = sizes
    features = 2 * ctx_size * dim
    c = lax.axis_index("ctx")
    z = lax.axis_index("pipe")
    side = lax.rem(z, 2)
    base = z - side
    top = base + 1
    other = base + 1 - side
    me = side * ctx_size + c

    def cols(head):
        return pl.ds(pl.multiple_of(head * dim, dim), dim)

    def rows(device):
        return pl.ds(pl.multiple_of(device * tokens, tokens), tokens)

    local = [
        pltpu.make_async_copy(tok_ref.at[0], own, local_sem.at[0]),
        pltpu.make_async_copy(tok_ref.at[0, :, cols(me)], stream.at[0, rows(c)], local_sem.at[1]),
    ]
    parts = []
    for q in range(2):
        head = q * ctx_size + c
        parts += [
            pltpu.make_async_copy(w_ref.at[0, head], raw.at[q], local_sem.at[2 + 3 * q]),
            pltpu.make_async_copy(gin_ref.at[:, cols(head)], gain_in.at[q], local_sem.at[3 + 3 * q]),
            pltpu.make_async_copy(gout_ref.at[:, cols(head)], gain_out.at[q], local_sem.at[4 + 3 * q]),
        ]
    for copy in local + parts:
        copy.start()

    peers = [(d, plane) for plane in (other, z) for d in (6, 7)]
    peers += [(d, plane) for plane in (other, z) for d in (2, 4, 3, 5)]
    peers += [(0, other), (1, other), (1, z)]
    barrier = pltpu.get_barrier_semaphore()
    for step in range(1, sections):
        plane = lax.rem(z + step, sections)
        pl.semaphore_signal(barrier, 1, device_id=(c, plane), device_id_type=MESH)
    for d in FAR_FIRST:
        pl.semaphore_signal(barrier, 1, device_id=(partner(c, d), z), device_id_type=MESH)

    def fold():
        for copy in parts:
            copy.wait()
        for q in range(2):
            across = gain_in[q]
            query = raw[q, :, :dim]
            key = raw[q, :, dim : 2 * dim]
            value = raw[q, :, 2 * dim :].astype(jnp.float32)
            crossed = lax.dot_general(
                key, query, (((1,), (1,)), ((), ())), preferred_element_type=jnp.float32
            )
            crossed = crossed * (across * dim ** (-0.5)) * lanes_to_rows(across)
            folded_maps[q, :dim] = crossed.astype(jnp.bfloat16)
            folded_maps[q, dim:] = (value.T * across).astype(jnp.bfloat16)
        weights[z] = folded_maps[side]
        gains[z] = gain_out[side]

    @pl.when(z == 0)
    def _():
        fold()

    local[0].wait()
    folded = jnp.zeros((tokens, 128), jnp.float32)
    for i in range(features // 128):
        piece = own[:, i * 128 : (i + 1) * 128].astype(jnp.float32)
        folded = folded + piece * piece
    total = jnp.sum(folded.T, 0, keepdims=True)
    which = lax.broadcasted_iota(jnp.int32, (ctx_size, tokens), 0)
    squares[0, me] = jnp.where(which == c, jnp.broadcast_to(total, (ctx_size, tokens)), 0.0)
    away = (1 - side) * ctx_size
    squares[0, pl.ds(away, ctx_size)] = jnp.zeros((ctx_size, ctx_size, tokens), jnp.float32)

    pl.semaphore_wait(barrier, ctx_size - 1 + sections - 1)

    def tok_copy(d):
        to = partner(c, d)
        return pltpu.make_async_remote_copy(
            tok_ref.at[0, :, cols(side * ctx_size + to)], stream.at[0, rows(c)],
            tok_send.at[0], tok_recv.at[d], device_id=(to, z), device_id_type=MESH,
        )

    def part(g):
        return pl.ds(sum(GROUPS[:g]), GROUPS[g])

    def first_sq_copy(d):
        return pltpu.make_async_remote_copy(
            squares.at[0, me], squares.at[0, me], sq_send.at[0, 0], sq_recv.at[0, 0],
            device_id=(partner(c, d), z), device_id_type=MESH,
        )

    def drain(every, sem):
        pltpu.make_async_copy(every, every, sem).wait()

    def first_sq_wait(sem):
        drain(squares.at[0, pl.ds(0, ctx_size - 1)], sem.at[0, 0])

    def sq_copy(layer, g, d, plane):
        return pltpu.make_async_remote_copy(
            squares.at[layer, me, part(g)], squares.at[layer, me, part(g)],
            sq_send.at[layer, g], sq_recv.at[layer, g],
            device_id=(partner(c, d), plane), device_id_type=MESH,
        )

    def sq_wait(sem, layer, g):
        drain(squares.at[layer, pl.ds(0, len(peers)), part(g)], sem.at[layer, g])

    def w_pieces(layer, q):
        return [
            (folded_maps.at[q, pl.ds(0, dim)], weights.at[layer, pl.ds(0, dim)]),
            (folded_maps.at[q, pl.ds(dim, dim)], weights.at[layer, pl.ds(dim, dim)]),
            (gain_out.at[q], gains.at[layer]),
        ]

    def w_copy(layer, to, i):
        source, target = w_pieces(layer, to % 2)[i]
        return pltpu.make_async_remote_copy(
            source, target, w_send.at[to, i], w_recv.at[layer, i],
            device_id=(c, to), device_id_type=MESH,
        )

    def send_weights(layer, *targets):
        for i in range(3):
            for to in targets:
                w_copy(layer, to, i).start()

    def weights_sent(layer, *targets):
        for to in targets:
            for i in range(3):
                w_copy(layer, to, i).wait_send()

    def await_piece(layer, i):
        source, target = w_pieces(layer, 0)[i]
        pltpu.make_async_remote_copy(
            source, target, w_send.at[0, i], w_recv.at[layer, i],
            device_id=(c, other), device_id_type=MESH,
        ).wait_recv()

    @pl.when(z == 0)
    def _():
        send_weights(0, 3, 2)

    for d in FAR_FIRST:
        tok_copy(d).start()
    for d in FAR_FIRST:
        first_sq_copy(d).start()
    pl.semaphore_signal(ready_sem, 1, device_id=(c, other), device_id_type=MESH)

    @pl.when(z > 0)
    def _():
        fold()

    for layer, to in ((1, 0), (2, 3), (3, 2)):
        @pl.when(z == layer)
        def _():
            send_weights(layer, to)

    at_row = lax.broadcasted_iota(jnp.int32, (tokens, tokens), 0)
    at_col = lax.broadcasted_iota(jnp.int32, (tokens, tokens), 1)
    causal = at_row <= at_col

    def out_copy(slot, plane, block):
        return pltpu.make_async_remote_copy(
            stream.at[slot, rows(block)], out_ref.at[0, 0, :, cols(me)],
            out_send.at[slot], out_recv.at[0],
            device_id=(block, plane), device_id_type=MESH,
        )

    def own_out(slot):
        return pltpu.make_async_copy(
            stream.at[slot, rows(c)], out_ref.at[0, 0, :, cols(me)], local_sem.at[0]
        )

    def send_out(slot, plane, blocks):
        for block in blocks:
            mine = jnp.logical_and(c == block, z == plane)

            @pl.when(jnp.logical_not(mine))
            def _():
                out_copy(slot, plane, block).start()

            @pl.when(mine)
            def _():
                own_out(slot).start()

    def attend(slot, block, exact, fine):
        queries = exact.astype(jnp.bfloat16)
        right[block, tokens:] = queries
        scores = product(stream[slot, rows(block)], queries)
        if fine:
            rest = (exact - queries.astype(jnp.float32)).astype(jnp.bfloat16)
            scores = scores + product(stream[slot, rows(block)], rest)
        right[block, :tokens] = jnp.where(causal, scores, 0.0).astype(jnp.bfloat16)

    def pair_of(pair):
        return jnp.concatenate([turned[2 * pair], turned[2 * pair + 1]], 1)

    def project(layer, slot, pair):
        projected = product(weights[layer], pair_of(pair))
        for i in range(2):
            here = projected[:, i * tokens : (i + 1) * tokens]
            left[2 * pair + i] = here[dim:]
            attend(slot, 2 * pair + i, here[:dim], pair + i == 0)

    def turn(block):
        turned[block] = stream[0, rows(block)].T

    def attend_first(block):
        attend(0, block, product(weights[0, :dim], turned[block]), True)

    def spread_gains(layer):
        gain_cols[...] = lanes_to_rows(gains[layer])

    def mix(layer, g):
        first = sum(GROUPS[:g])
        span = GROUPS[g]
        slot = lax.rem(layer, 2)

        @pl.when(layer > 0)
        def _():
            sq_wait(sq_recv, layer, g)

        mean = jnp.sum(squares[layer, :, first : first + span], 0) * (1.0 / features)
        scale = lax.rsqrt(mean + epsilon)
        twice = scale * scale
        sums = []
        running = state[...] if g else jnp.zeros((dim, dim), jnp.float32)
        for i in range(span):
            block = first + i
            own_scale, own_twice = scale[i : i + 1], twice[i : i + 1]
            scaled = (left[block] * own_twice).astype(jnp.bfloat16)
            mixed = product(
                jnp.concatenate([scaled, running.astype(jnp.bfloat16)], 1), right[block]
            )
            if block + 1 < ctx_size:
                running = running + product(scaled, stream[slot, rows(block)])
            power = jnp.sum(mixed * mixed, 0, keepdims=True) * (1.0 / dim)
            factor = own_scale * lax.rsqrt(own_twice * power + epsilon)
            leaving = turned[block].astype(jnp.float32) + gain_cols[...] * (mixed * factor)
            rounded = leaving.astype(jnp.bfloat16)
            turned[block] = rounded
            stream[1 - slot, rows(block)] = rounded.T
            sums.append(jnp.sum(leaving * leaving, 0, keepdims=True))
        if g + 1 < len(GROUPS):
            state[...] = running
        squares[layer + 1, me, first : first + span] = jnp.concatenate(sums, 0)

        @pl.when(layer < top)
        def _():
            for d, plane in peers:
                sq_copy(layer + 1, g, d, plane).start()

        @pl.when(layer == top)
        def _():
            send_out(0, top, range(first, first + span))

        if g + 1 == len(GROUPS):
            @pl.when(layer == base)
            def _():
                send_out(1, base, range(ctx_size))

    @pl.when(z == 1)
    def _():
        send_weights(1, 3, 2)

    @pl.when(z == 0)
    def _():
        weights_sent(0, 3, 2)
        send_weights(0, 1)

    def await_first(i):
        @pl.when(z > 0)
        def _():
            await_piece(0, i)

    def arrive(pair):
        for d in pair:
            tok_copy(d).wait_recv()
        for d in pair:
            turn(partner(c, d))

    local[1].wait()
    turn(c)
    arrive((1,))
    arrive((6, 7))
    await_first(0)
    for d in (0, 1, 6, 7):
        attend_first(partner(c, d))
    for pair in ((2, 4), (3, 5)):
        arrive(pair)
        for d in pair:
            attend_first(partner(c, d))
    await_first(1)
    for pair in range(ctx_size // 2):
        values = product(weights[0, dim:], pair_of(pair))
        for i in range(2):
            left[2 * pair + i] = values[:, i * tokens : (i + 1) * tokens]
    await_first(2)
    spread_gains(0)

    first_sq_wait(sq_recv)
    pl.semaphore_wait(ready_sem, 1)

    def one_layer(layer, carry):
        for g in range(len(GROUPS)):
            mix(layer, g)

        @pl.when(layer < top)
        def _():
            @pl.when(layer + 1 != z)
            def _():
                for i in range(3):
                    await_piece(layer + 1, i)

            spread_gains(layer + 1)
            for pair in range(ctx_size // 2):
                project(layer + 1, lax.rem(layer + 1, 2), pair)

        @pl.when(layer > 0)
        def _():
            for g in range(len(GROUPS)):
                sq_wait(sq_send, layer, g)

        return carry

    lax.fori_loop(0, base + 2, one_layer, 0)

    first_sq_wait(sq_send)
    drain(stream.at[0, pl.ds(0, (ctx_size - 1) * tokens)], tok_send.at[0])
    for layer, targets in ((0, (1,)), (1, (3, 2, 0)), (2, (3,)), (3, (2,))):
        @pl.when(z == layer)
        def _():
            weights_sent(layer, *targets)

    for slot, plane in ((1, base), (0, top)):
        @pl.when(z == plane)
        def _():
            drain(stream.at[slot, pl.ds(0, (ctx_size - 1) * tokens)], out_send.at[slot])
            own_out(slot).wait()

        @pl.when(z != plane)
        def _():
            drain(stream.at[slot], out_send.at[slot])

    drain(out_ref.at[0, 0, :, pl.ds(0, len(peers) * dim)], out_recv.at[0])


def relay(tokens, w_qkv, norm_gain, out_gain):
    ctx_size, sections = lax.axis_size("ctx"), lax.axis_size("pipe")
    rows, features = tokens.shape[1:]
    dim = w_qkv.shape[2]
    length = ctx_size * rows
    dma = pltpu.SemaphoreType.DMA
    return pl.pallas_call(
        functools.partial(relay_kernel, (ctx_size, sections, dim, rows)),
        out_shape=pltpu.VMEM((1,) + tokens.shape, jnp.bfloat16),
        in_specs=[pl.BlockSpec(memory_space=pl.ANY)] * 4,
        out_specs=pl.BlockSpec(memory_space=pltpu.VMEM),
        scratch_shapes=[
            pltpu.VMEM((rows, features), jnp.bfloat16),
            pltpu.VMEM((2, length, dim), jnp.bfloat16),
            pltpu.VMEM((ctx_size, dim, rows), jnp.bfloat16),
            pltpu.VMEM((2, dim, 3 * dim), jnp.bfloat16),
            pltpu.VMEM((2, 1, dim), jnp.float32),
            pltpu.VMEM((2, 1, dim), jnp.float32),
            pltpu.VMEM((2, 2 * dim, dim), jnp.bfloat16),
            pltpu.VMEM((sections, 2 * dim, dim), jnp.bfloat16),
            pltpu.VMEM((sections, 1, dim), jnp.float32),
            pltpu.VMEM((dim, rows), jnp.float32),
            pltpu.VMEM((ctx_size, dim, rows), jnp.float32),
            pltpu.VMEM((ctx_size, rows + dim, rows), jnp.bfloat16),
            pltpu.VMEM((dim, dim), jnp.float32),
            pltpu.VMEM((sections + 1, 2 * ctx_size, ctx_size, rows), jnp.float32),
            pltpu.SemaphoreType.REGULAR,
            dma((8,)),
            dma((1,)),
            dma((ctx_size,)),
            dma((sections, len(GROUPS))),
            dma((sections, len(GROUPS))),
            dma((sections, 3)),
            dma((sections, 3)),
            dma((2,)),
            dma((1,)),
        ],
        compiler_params=pltpu.CompilerParams(collective_id=0, has_side_effects=True),
    )(tokens, w_qkv, norm_gain, out_gain)


def solution(mesh):
    ctx_size, sections = mesh.shape["ctx"], mesh.shape["pipe"]

    def body(tokens, w_qkv, norm_gain, out_gain):
        micro_count, rows = tokens.shape[:2]
        fits = (
            ctx_size == 8
            and sections == 4
            and micro_count == 1
            and rows == 128
            and w_qkv.shape[1] == 2 * ctx_size
            and w_qkv.shape[2] == 128
        )
        return (relay if fits else shards)(tokens, w_qkv, norm_gain, out_gain)

    placed = (P(None, "ctx", None), P("pipe", None, None, None), P("pipe", None), P("pipe", None))
    return jax.shard_map(
        body, mesh=mesh, in_specs=placed, out_specs=P("pipe", None, "ctx", None), check_vma=False
    )
```

```python
import functools

import jax
import jax.numpy as jnp
from jax import lax
from jax.experimental import pallas as pl
from jax.experimental.pallas import tpu as pltpu
from jax.sharding import PartitionSpec as P

epsilon = 1e-06


def shifted(block, axis, distance):
    devices = range(lax.axis_size(axis))
    route = [(i - distance, i) for i in devices if i - distance in devices]
    return lax.ppermute(block, axis, route)


def run_layer(stream, gain_in, weights, gain_out):
    row_count = stream.shape[0]
    head_count = weights.shape[0]
    head_dim = weights.shape[1]
    widened = stream.astype(jnp.float32)
    normed = (
        widened * lax.rsqrt(jnp.mean(widened * widened, -1, keepdims=True) + epsilon) * gain_in
    ).astype(jnp.bfloat16)
    projected = jnp.einsum(
        "thd,hde->hte",
        normed.reshape(row_count, head_count, head_dim),
        weights,
        preferred_element_type=jnp.float32,
    )
    queries = (projected[..., :head_dim] * head_dim ** (-0.5)).astype(jnp.bfloat16)
    keys_local = projected[..., head_dim : 2 * head_dim].astype(jnp.bfloat16)
    values_local = projected[..., 2 * head_dim :].astype(jnp.bfloat16)
    kv_state = jnp.einsum(
        "hte,htf->hef", keys_local, values_local, preferred_element_type=jnp.float32
    )
    flat_state = kv_state.reshape(1, head_count * head_dim, head_dim)
    spread = lax.all_to_all(
        flat_state.astype(jnp.bfloat16), "ctx", split_axis=1, concat_axis=0, tiled=True
    ).astype(flat_state.dtype)
    running = jnp.cumsum(spread, axis=0)
    lower = jnp.concatenate([jnp.zeros_like(spread[:1]), running[:-1]], axis=0)
    returned = lax.all_to_all(
        lower.astype(jnp.bfloat16), "ctx", split_axis=0, concat_axis=1, tiled=True
    ).astype(lower.dtype)
    prefix = returned.reshape(kv_state.shape)
    scores = jnp.einsum("hte,hse->hts", queries, keys_local, preferred_element_type=jnp.float32)
    positions = jnp.arange(row_count, dtype=jnp.int32)
    causal = positions[:, None] >= positions[None, :]
    masked = jnp.where(causal, scores, 0.0).astype(jnp.bfloat16)
    mixed_heads = jnp.einsum(
        "hts,hsf->htf", masked, values_local, preferred_element_type=jnp.float32
    )
    mixed_heads = mixed_heads + jnp.einsum(
        "hte,hef->htf", queries, prefix.astype(jnp.bfloat16), preferred_element_type=jnp.float32
    )
    mixed_heads = mixed_heads * lax.rsqrt(
        jnp.mean(mixed_heads * mixed_heads, -1, keepdims=True) + epsilon
    )
    branch = jnp.transpose(mixed_heads, (1, 0, 2)).reshape(row_count, head_count * head_dim)
    return (widened + branch * gain_out).astype(jnp.bfloat16)


def shards(tokens, w_qkv, norm_gain, out_gain):
    section_count = lax.axis_size("pipe")
    section_index = lax.axis_index("pipe")
    micro_count = tokens.shape[0]
    hidden_buffer = jnp.zeros(tokens.shape, jnp.bfloat16)
    carried = jnp.zeros(tokens.shape[1:], jnp.bfloat16)
    total_steps = micro_count + section_count - 1
    for tick_index in range(total_steps):
        fresh = tokens[min(tick_index, micro_count - 1)]
        layer_input = jnp.where(section_index == 0, fresh, carried)
        result = run_layer(layer_input, norm_gain[0], w_qkv[0], out_gain[0])
        micro_index = tick_index - section_index
        usable = (micro_index >= 0) & (micro_index < micro_count)
        slot_index = jnp.clip(micro_index, 0, micro_count - 1)
        previous = lax.dynamic_index_in_dim(hidden_buffer, slot_index, 0, keepdims=False)
        hidden_buffer = lax.dynamic_update_index_in_dim(
            hidden_buffer, jnp.where(usable, result, previous), slot_index, 0
        )
        if tick_index + 1 < total_steps:
            carried = shifted(result, "pipe", 1)
    return hidden_buffer[None]


MESH = pl.DeviceIdType.MESH
FAR_FIRST = (6, 7, 2, 4, 3, 5, 1)


def partner(index, flips):
    total = 0
    for bit in (1, 2, 4):
        own = lax.rem(index // bit, 2)
        total = total + (lax.rem(own + 1, 2) if flips & bit else own) * bit
    return total


def lanes_to_rows(row):
    return jnp.broadcast_to(row, (128, row.shape[1])).T


def product(a, b):
    return jnp.dot(a, b, preferred_element_type=jnp.float32)


GROUPS = (3, 3, 2)


def relay_kernel(
    sizes,
    tok_ref,
    w_ref,
    gin_ref,
    gout_ref,
    out_ref,
    own,
    stream,
    turned,
    raw,
    gain_in,
    gain_out,
    folded_maps,
    weights,
    gains,
    gain_cols,
    left,
    right,
    state,
    squares,
    ready_sem,
    local_sem,
    tok_send,
    tok_recv,
    sq_send,
    sq_recv,
    w_send,
    w_recv,
    out_send,
    out_recv,
):
    ctx_size, sections, dim, tokens = sizes
    features = 2 * ctx_size * dim
    c = lax.axis_index("ctx")
    z = lax.axis_index("pipe")
    side = lax.rem(z, 2)
    base = z - side
    top = base + 1
    other = base + 1 - side
    me = side * ctx_size + c

    def cols(head):
        return pl.ds(pl.multiple_of(head * dim, dim), dim)

    def rows(device):
        return pl.ds(pl.multiple_of(device * tokens, tokens), tokens)

    local = [
        pltpu.make_async_copy(tok_ref.at[0], own, local_sem.at[0]),
        pltpu.make_async_copy(tok_ref.at[0, :, cols(me)], stream.at[0, rows(c)], local_sem.at[1]),
    ]
    parts = []
    for q in range(2):
        head = q * ctx_size + c
        parts += [
            pltpu.make_async_copy(w_ref.at[0, head], raw.at[q], local_sem.at[2 + 3 * q]),
            pltpu.make_async_copy(gin_ref.at[:, cols(head)], gain_in.at[q], local_sem.at[3 + 3 * q]),
            pltpu.make_async_copy(gout_ref.at[:, cols(head)], gain_out.at[q], local_sem.at[4 + 3 * q]),
        ]
    for copy in local + parts:
        copy.start()

    peers = [(d, plane) for plane in (other, z) for d in (6, 7)]
    peers += [(d, plane) for plane in (other, z) for d in (2, 4, 3, 5)]
    peers += [(0, other), (1, other), (1, z)]
    barrier = pltpu.get_barrier_semaphore()
    for step in range(1, sections):
        plane = lax.rem(z + step, sections)
        pl.semaphore_signal(barrier, 1, device_id=(c, plane), device_id_type=MESH)
    for d in FAR_FIRST:
        pl.semaphore_signal(barrier, 1, device_id=(partner(c, d), z), device_id_type=MESH)

    def fold():
        for copy in parts:
            copy.wait()
        for q in range(2):
            across = gain_in[q]
            query = raw[q, :, :dim]
            key = raw[q, :, dim : 2 * dim]
            value = raw[q, :, 2 * dim :].astype(jnp.float32)
            crossed = lax.dot_general(
                key, query, (((1,), (1,)), ((), ())), preferred_element_type=jnp.float32
            )
            crossed = crossed * (across * dim ** (-0.5)) * lanes_to_rows(across)
            folded_maps[q, :dim] = crossed.astype(jnp.bfloat16)
            folded_maps[q, dim:] = (value.T * across).astype(jnp.bfloat16)
        weights[z] = folded_maps[side]
        gains[z] = gain_out[side]

    @pl.when(z == 0)
    def _():
        fold()

    local[0].wait()
    folded = jnp.zeros((tokens, 128), jnp.float32)
    for i in range(features // 128):
        piece = own[:, i * 128 : (i + 1) * 128].astype(jnp.float32)
        folded = folded + piece * piece
    total = jnp.sum(folded.T, 0, keepdims=True)
    which = lax.broadcasted_iota(jnp.int32, (ctx_size, tokens), 0)
    squares[0, me] = jnp.where(which == c, jnp.broadcast_to(total, (ctx_size, tokens)), 0.0)
    away = (1 - side) * ctx_size
    squares[0, pl.ds(away, ctx_size)] = jnp.zeros((ctx_size, ctx_size, tokens), jnp.float32)

    pl.semaphore_wait(barrier, ctx_size - 1 + sections - 1)

    def tok_copy(d):
        to = partner(c, d)
        return pltpu.make_async_remote_copy(
            tok_ref.at[0, :, cols(side * ctx_size + to)], stream.at[0, rows(c)],
            tok_send.at[0], tok_recv.at[d], device_id=(to, z), device_id_type=MESH,
        )

    def part(g):
        return pl.ds(sum(GROUPS[:g]), GROUPS[g])

    def first_sq_copy(d):
        return pltpu.make_async_remote_copy(
            squares.at[0, me], squares.at[0, me], sq_send.at[0, 0], sq_recv.at[0, 0],
            device_id=(partner(c, d), z), device_id_type=MESH,
        )

    def drain(every, sem):
        pltpu.make_async_copy(every, every, sem).wait()

    def first_sq_wait(sem):
        drain(squares.at[0, pl.ds(0, ctx_size - 1)], sem.at[0, 0])

    def sq_copy(layer, g, d, plane):
        return pltpu.make_async_remote_copy(
            squares.at[layer, me, part(g)], squares.at[layer, me, part(g)],
            sq_send.at[layer, g], sq_recv.at[layer, g],
            device_id=(partner(c, d), plane), device_id_type=MESH,
        )

    def sq_wait(sem, layer, g):
        drain(squares.at[layer, pl.ds(0, len(peers)), part(g)], sem.at[layer, g])

    def w_pieces(layer, q):
        return [
            (folded_maps.at[q, pl.ds(0, dim)], weights.at[layer, pl.ds(0, dim)]),
            (folded_maps.at[q, pl.ds(dim, dim)], weights.at[layer, pl.ds(dim, dim)]),
            (gain_out.at[q], gains.at[layer]),
        ]

    def w_copy(layer, to, i):
        source, target = w_pieces(layer, to % 2)[i]
        return pltpu.make_async_remote_copy(
            source, target, w_send.at[to, i], w_recv.at[layer, i],
            device_id=(c, to), device_id_type=MESH,
        )

    def send_weights(layer, *targets):
        for i in range(3):
            for to in targets:
                w_copy(layer, to, i).start()

    def weights_sent(layer, *targets):
        for to in targets:
            for i in range(3):
                w_copy(layer, to, i).wait_send()

    def await_piece(layer, i):
        source, target = w_pieces(layer, 0)[i]
        pltpu.make_async_remote_copy(
            source, target, w_send.at[0, i], w_recv.at[layer, i],
            device_id=(c, other), device_id_type=MESH,
        ).wait_recv()

    @pl.when(z == 0)
    def _():
        send_weights(0, 3, 2)

    for d in FAR_FIRST:
        tok_copy(d).start()
    for d in FAR_FIRST:
        first_sq_copy(d).start()
    pl.semaphore_signal(ready_sem, 1, device_id=(c, other), device_id_type=MESH)

    @pl.when(z > 0)
    def _():
        fold()

    for layer, to in ((1, 0), (2, 3), (3, 2)):
        @pl.when(z == layer)
        def _():
            send_weights(layer, to)

    at_row = lax.broadcasted_iota(jnp.int32, (tokens, tokens), 0)
    at_col = lax.broadcasted_iota(jnp.int32, (tokens, tokens), 1)
    causal = at_row <= at_col

    def out_copy(slot, plane, block):
        return pltpu.make_async_remote_copy(
            stream.at[slot, rows(block)], out_ref.at[0, 0, :, cols(me)],
            out_send.at[slot], out_recv.at[0],
            device_id=(block, plane), device_id_type=MESH,
        )

    def own_out(slot):
        return pltpu.make_async_copy(
            stream.at[slot, rows(c)], out_ref.at[0, 0, :, cols(me)], local_sem.at[0]
        )

    def send_out(slot, plane, blocks):
        for block in reversed(blocks):
            mine = jnp.logical_and(c == block, z == plane)

            @pl.when(jnp.logical_not(mine))
            def _():
                out_copy(slot, plane, block).start()

            @pl.when(mine)
            def _():
                own_out(slot).start()

    def attend(slot, block, exact, fine):
        queries = exact.astype(jnp.bfloat16)
        right[block, tokens:] = queries
        scores = product(stream[slot, rows(block)], queries)
        if fine:
            rest = (exact - queries.astype(jnp.float32)).astype(jnp.bfloat16)
            scores = scores + product(stream[slot, rows(block)], rest)
        right[block, :tokens] = jnp.where(causal, scores, 0.0).astype(jnp.bfloat16)

    def pair_of(pair):
        return jnp.concatenate([turned[2 * pair], turned[2 * pair + 1]], 1)

    def project(layer, slot, pair):
        projected = product(weights[layer], pair_of(pair))
        for i in range(2):
            here = projected[:, i * tokens : (i + 1) * tokens]
            left[2 * pair + i] = here[dim:]
            attend(slot, 2 * pair + i, here[:dim], pair + i == 0)

    def turn(block):
        turned[block] = stream[0, rows(block)].T

    def attend_first(block):
        attend(0, block, product(weights[0, :dim], turned[block]), True)

    def spread_gains(layer):
        gain_cols[...] = lanes_to_rows(gains[layer])

    def mix(layer, g):
        first = sum(GROUPS[:g])
        span = GROUPS[g]
        slot = lax.rem(layer, 2)

        @pl.when(layer > 0)
        def _():
            sq_wait(sq_recv, layer, g)

        mean = jnp.sum(squares[layer, :, first : first + span], 0) * (1.0 / features)
        scale = lax.rsqrt(mean + epsilon)
        twice = scale * scale
        sums = []
        running = state[...] if g else jnp.zeros((dim, dim), jnp.float32)
        for i in range(span):
            block = first + i
            own_scale, own_twice = scale[i : i + 1], twice[i : i + 1]
            scaled = (left[block] * own_twice).astype(jnp.bfloat16)
            mixed = product(
                jnp.concatenate([scaled, running.astype(jnp.bfloat16)], 1), right[block]
            )
            if block + 1 < ctx_size:
                running = running + product(scaled, stream[slot, rows(block)])
            power = jnp.sum(mixed * mixed, 0, keepdims=True) * (1.0 / dim)
            factor = own_scale * lax.rsqrt(own_twice * power + epsilon)
            leaving = turned[block].astype(jnp.float32) + gain_cols[...] * (mixed * factor)
            rounded = leaving.astype(jnp.bfloat16)
            turned[block] = rounded
            stream[1 - slot, rows(block)] = rounded.T
            sums.append(jnp.sum(leaving * leaving, 0, keepdims=True))
        if g + 1 < len(GROUPS):
            state[...] = running
        squares[layer + 1, me, first : first + span] = jnp.concatenate(sums, 0)

        @pl.when(layer < top)
        def _():
            for d, plane in peers:
                sq_copy(layer + 1, g, d, plane).start()

        @pl.when(layer == top)
        def _():
            send_out(0, top, range(first, first + span))

        if g + 1 == len(GROUPS):
            @pl.when(layer == base)
            def _():
                send_out(1, base, range(ctx_size))

    @pl.when(z == 1)
    def _():
        send_weights(1, 3, 2)

    @pl.when(z == 0)
    def _():
        weights_sent(0, 3, 2)
        send_weights(0, 1)

    def await_first(i):
        @pl.when(z > 0)
        def _():
            await_piece(0, i)

    def arrive(pair):
        for d in pair:
            tok_copy(d).wait_recv()
        for d in pair:
            turn(partner(c, d))

    local[1].wait()
    turn(c)
    arrive((1,))
    arrive((6, 7))
    await_first(0)
    for d in (0, 1, 6, 7):
        attend_first(partner(c, d))
    for pair in ((2, 4), (3, 5)):
        arrive(pair)
        for d in pair:
            attend_first(partner(c, d))
    await_first(1)
    for pair in range(ctx_size // 2):
        values = product(weights[0, dim:], pair_of(pair))
        for i in range(2):
            left[2 * pair + i] = values[:, i * tokens : (i + 1) * tokens]
    await_first(2)
    spread_gains(0)

    first_sq_wait(sq_recv)
    pl.semaphore_wait(ready_sem, 1)

    def one_layer(layer, carry):
        for g in range(len(GROUPS)):
            mix(layer, g)

        @pl.when(layer < top)
        def _():
            @pl.when(layer + 1 != z)
            def _():
                for i in range(3):
                    await_piece(layer + 1, i)

            spread_gains(layer + 1)
            for pair in range(ctx_size // 2):
                project(layer + 1, lax.rem(layer + 1, 2), pair)

        @pl.when(layer > 0)
        def _():
            for g in range(len(GROUPS)):
                sq_wait(sq_send, layer, g)

        return carry

    lax.fori_loop(0, base + 2, one_layer, 0)

    first_sq_wait(sq_send)
    drain(stream.at[0, pl.ds(0, (ctx_size - 1) * tokens)], tok_send.at[0])
    for layer, targets in ((0, (1,)), (1, (3, 2, 0)), (2, (3,)), (3, (2,))):
        @pl.when(z == layer)
        def _():
            weights_sent(layer, *targets)

    for slot, plane in ((1, base), (0, top)):
        @pl.when(z == plane)
        def _():
            drain(stream.at[slot, pl.ds(0, (ctx_size - 1) * tokens)], out_send.at[slot])
            own_out(slot).wait()

        @pl.when(z != plane)
        def _():
            drain(stream.at[slot], out_send.at[slot])

    drain(out_ref.at[0, 0, :, pl.ds(0, len(peers) * dim)], out_recv.at[0])


def relay(tokens, w_qkv, norm_gain, out_gain):
    ctx_size, sections = lax.axis_size("ctx"), lax.axis_size("pipe")
    rows, features = tokens.shape[1:]
    dim = w_qkv.shape[2]
    length = ctx_size * rows
    dma = pltpu.SemaphoreType.DMA
    return pl.pallas_call(
        functools.partial(relay_kernel, (ctx_size, sections, dim, rows)),
        out_shape=pltpu.VMEM((1,) + tokens.shape, jnp.bfloat16),
        in_specs=[pl.BlockSpec(memory_space=pl.ANY)] * 4,
        out_specs=pl.BlockSpec(memory_space=pltpu.VMEM),
        scratch_shapes=[
            pltpu.VMEM((rows, features), jnp.bfloat16),
            pltpu.VMEM((2, length, dim), jnp.bfloat16),
            pltpu.VMEM((ctx_size, dim, rows), jnp.bfloat16),
            pltpu.VMEM((2, dim, 3 * dim), jnp.bfloat16),
            pltpu.VMEM((2, 1, dim), jnp.float32),
            pltpu.VMEM((2, 1, dim), jnp.float32),
            pltpu.VMEM((2, 2 * dim, dim), jnp.bfloat16),
            pltpu.VMEM((sections, 2 * dim, dim), jnp.bfloat16),
            pltpu.VMEM((sections, 1, dim), jnp.float32),
            pltpu.VMEM((dim, rows), jnp.float32),
            pltpu.VMEM((ctx_size, dim, rows), jnp.float32),
            pltpu.VMEM((ctx_size, rows + dim, rows), jnp.bfloat16),
            pltpu.VMEM((dim, dim), jnp.float32),
            pltpu.VMEM((sections + 1, 2 * ctx_size, ctx_size, rows), jnp.float32),
            pltpu.SemaphoreType.REGULAR,
            dma((8,)),
            dma((1,)),
            dma((ctx_size,)),
            dma((sections, len(GROUPS))),
            dma((sections, len(GROUPS))),
            dma((sections, 3)),
            dma((sections, 3)),
            dma((2,)),
            dma((1,)),
        ],
        compiler_params=pltpu.CompilerParams(collective_id=0, has_side_effects=True),
    )(tokens, w_qkv, norm_gain, out_gain)


def solution(mesh):
    ctx_size, sections = mesh.shape["ctx"], mesh.shape["pipe"]

    def body(tokens, w_qkv, norm_gain, out_gain):
        micro_count, rows = tokens.shape[:2]
        fits = (
            ctx_size == 8
            and sections == 4
            and micro_count == 1
            and rows == 128
            and w_qkv.shape[1] == 2 * ctx_size
            and w_qkv.shape[2] == 128
        )
        return (relay if fits else shards)(tokens, w_qkv, norm_gain, out_gain)

    placed = (P(None, "ctx", None), P("pipe", None, None, None), P("pipe", None), P("pipe", None))
    return jax.shard_map(
        body, mesh=mesh, in_specs=placed, out_specs=P("pipe", None, "ctx", None), check_vma=False
    )
```

```python
import functools

import jax
import jax.numpy as jnp
from jax import lax
from jax.experimental import pallas as pl
from jax.experimental.pallas import tpu as pltpu
from jax.sharding import PartitionSpec as P

epsilon = 1e-06


def shifted(block, axis, distance):
    devices = range(lax.axis_size(axis))
    route = [(i - distance, i) for i in devices if i - distance in devices]
    return lax.ppermute(block, axis, route)


def run_layer(stream, gain_in, weights, gain_out):
    row_count = stream.shape[0]
    head_count = weights.shape[0]
    head_dim = weights.shape[1]
    widened = stream.astype(jnp.float32)
    normed = (
        widened * lax.rsqrt(jnp.mean(widened * widened, -1, keepdims=True) + epsilon) * gain_in
    ).astype(jnp.bfloat16)
    projected = jnp.einsum(
        "thd,hde->hte",
        normed.reshape(row_count, head_count, head_dim),
        weights,
        preferred_element_type=jnp.float32,
    )
    queries = (projected[..., :head_dim] * head_dim ** (-0.5)).astype(jnp.bfloat16)
    keys_local = projected[..., head_dim : 2 * head_dim].astype(jnp.bfloat16)
    values_local = projected[..., 2 * head_dim :].astype(jnp.bfloat16)
    kv_state = jnp.einsum(
        "hte,htf->hef", keys_local, values_local, preferred_element_type=jnp.float32
    )
    flat_state = kv_state.reshape(1, head_count * head_dim, head_dim)
    spread = lax.all_to_all(
        flat_state.astype(jnp.bfloat16), "ctx", split_axis=1, concat_axis=0, tiled=True
    ).astype(flat_state.dtype)
    running = jnp.cumsum(spread, axis=0)
    lower = jnp.concatenate([jnp.zeros_like(spread[:1]), running[:-1]], axis=0)
    returned = lax.all_to_all(
        lower.astype(jnp.bfloat16), "ctx", split_axis=0, concat_axis=1, tiled=True
    ).astype(lower.dtype)
    prefix = returned.reshape(kv_state.shape)
    scores = jnp.einsum("hte,hse->hts", queries, keys_local, preferred_element_type=jnp.float32)
    positions = jnp.arange(row_count, dtype=jnp.int32)
    causal = positions[:, None] >= positions[None, :]
    masked = jnp.where(causal, scores, 0.0).astype(jnp.bfloat16)
    mixed_heads = jnp.einsum(
        "hts,hsf->htf", masked, values_local, preferred_element_type=jnp.float32
    )
    mixed_heads = mixed_heads + jnp.einsum(
        "hte,hef->htf", queries, prefix.astype(jnp.bfloat16), preferred_element_type=jnp.float32
    )
    mixed_heads = mixed_heads * lax.rsqrt(
        jnp.mean(mixed_heads * mixed_heads, -1, keepdims=True) + epsilon
    )
    branch = jnp.transpose(mixed_heads, (1, 0, 2)).reshape(row_count, head_count * head_dim)
    return (widened + branch * gain_out).astype(jnp.bfloat16)


def shards(tokens, w_qkv, norm_gain, out_gain):
    section_count = lax.axis_size("pipe")
    section_index = lax.axis_index("pipe")
    micro_count = tokens.shape[0]
    hidden_buffer = jnp.zeros(tokens.shape, jnp.bfloat16)
    carried = jnp.zeros(tokens.shape[1:], jnp.bfloat16)
    total_steps = micro_count + section_count - 1
    for tick_index in range(total_steps):
        fresh = tokens[min(tick_index, micro_count - 1)]
        layer_input = jnp.where(section_index == 0, fresh, carried)
        result = run_layer(layer_input, norm_gain[0], w_qkv[0], out_gain[0])
        micro_index = tick_index - section_index
        usable = (micro_index >= 0) & (micro_index < micro_count)
        slot_index = jnp.clip(micro_index, 0, micro_count - 1)
        previous = lax.dynamic_index_in_dim(hidden_buffer, slot_index, 0, keepdims=False)
        hidden_buffer = lax.dynamic_update_index_in_dim(
            hidden_buffer, jnp.where(usable, result, previous), slot_index, 0
        )
        if tick_index + 1 < total_steps:
            carried = shifted(result, "pipe", 1)
    return hidden_buffer[None]


MESH = pl.DeviceIdType.MESH
FAR_FIRST = (6, 7, 2, 4, 3, 5, 1)


def partner(index, flips):
    total = 0
    for bit in (1, 2, 4):
        own = lax.rem(index // bit, 2)
        total = total + (lax.rem(own + 1, 2) if flips & bit else own) * bit
    return total


def lanes_to_rows(row):
    return jnp.broadcast_to(row, (128, row.shape[1])).T


def product(a, b):
    return jnp.dot(a, b, preferred_element_type=jnp.float32)


GROUPS = (1, 2, 2, 3)


def relay_kernel(
    sizes,
    tok_ref,
    w_ref,
    gin_ref,
    gout_ref,
    out_ref,
    own,
    stream,
    turned,
    raw,
    gain_in,
    gain_out,
    folded_maps,
    weights,
    gains,
    gain_cols,
    left,
    right,
    state,
    squares,
    ready_sem,
    local_sem,
    tok_send,
    tok_recv,
    sq_send,
    sq_recv,
    w_send,
    w_recv,
    out_send,
    out_recv,
):
    ctx_size, sections, dim, tokens = sizes
    features = 2 * ctx_size * dim
    c = lax.axis_index("ctx")
    z = lax.axis_index("pipe")
    side = lax.rem(z, 2)
    base = z - side
    top = base + 1
    other = base + 1 - side
    me = side * ctx_size + c

    def cols(head):
        return pl.ds(pl.multiple_of(head * dim, dim), dim)

    def rows(device):
        return pl.ds(pl.multiple_of(device * tokens, tokens), tokens)

    local = [
        pltpu.make_async_copy(tok_ref.at[0], own, local_sem.at[0]),
        pltpu.make_async_copy(tok_ref.at[0, :, cols(me)], stream.at[0, rows(c)], local_sem.at[1]),
    ]
    parts = []
    for q in range(2):
        head = q * ctx_size + c
        parts += [
            pltpu.make_async_copy(w_ref.at[0, head], raw.at[q], local_sem.at[2 + 3 * q]),
            pltpu.make_async_copy(gin_ref.at[:, cols(head)], gain_in.at[q], local_sem.at[3 + 3 * q]),
            pltpu.make_async_copy(gout_ref.at[:, cols(head)], gain_out.at[q], local_sem.at[4 + 3 * q]),
        ]
    for copy in local + parts:
        copy.start()

    peers = [(d, plane) for plane in (other, z) for d in (6, 7)]
    peers += [(d, plane) for plane in (other, z) for d in (2, 4, 3, 5)]
    peers += [(0, other), (1, other), (1, z)]
    barrier = pltpu.get_barrier_semaphore()
    for step in range(1, sections):
        plane = lax.rem(z + step, sections)
        pl.semaphore_signal(barrier, 1, device_id=(c, plane), device_id_type=MESH)
    for d in FAR_FIRST:
        pl.semaphore_signal(barrier, 1, device_id=(partner(c, d), z), device_id_type=MESH)

    def fold():
        for copy in parts:
            copy.wait()
        for q in range(2):
            across = gain_in[q]
            query = raw[q, :, :dim]
            key = raw[q, :, dim : 2 * dim]
            value = raw[q, :, 2 * dim :].astype(jnp.float32)
            crossed = lax.dot_general(
                key, query, (((1,), (1,)), ((), ())), preferred_element_type=jnp.float32
            )
            crossed = crossed * (across * dim ** (-0.5)) * lanes_to_rows(across)
            folded_maps[q, :dim] = crossed.astype(jnp.bfloat16)
            folded_maps[q, dim:] = (value.T * across).astype(jnp.bfloat16)
        weights[z] = folded_maps[side]
        gains[z] = gain_out[side]

    @pl.when(z == 0)
    def _():
        fold()

    local[0].wait()
    folded = jnp.zeros((tokens, 128), jnp.float32)
    for i in range(features // 128):
        piece = own[:, i * 128 : (i + 1) * 128].astype(jnp.float32)
        folded = folded + piece * piece
    total = jnp.sum(folded.T, 0, keepdims=True)
    which = lax.broadcasted_iota(jnp.int32, (ctx_size, tokens), 0)
    squares[0, me] = jnp.where(which == c, jnp.broadcast_to(total, (ctx_size, tokens)), 0.0)
    away = (1 - side) * ctx_size
    squares[0, pl.ds(away, ctx_size)] = jnp.zeros((ctx_size, ctx_size, tokens), jnp.float32)

    pl.semaphore_wait(barrier, ctx_size - 1 + sections - 1)

    def tok_copy(d):
        to = partner(c, d)
        return pltpu.make_async_remote_copy(
            tok_ref.at[0, :, cols(side * ctx_size + to)], stream.at[0, rows(c)],
            tok_send.at[0], tok_recv.at[d], device_id=(to, z), device_id_type=MESH,
        )

    def part(g):
        return pl.ds(sum(GROUPS[:g]), GROUPS[g])

    def first_sq_copy(d):
        return pltpu.make_async_remote_copy(
            squares.at[0, me], squares.at[0, me], sq_send.at[0, 0], sq_recv.at[0, 0],
            device_id=(partner(c, d), z), device_id_type=MESH,
        )

    def drain(every, sem):
        pltpu.make_async_copy(every, every, sem).wait()

    def first_sq_wait(sem):
        drain(squares.at[0, pl.ds(0, ctx_size - 1)], sem.at[0, 0])

    def sq_copy(layer, g, d, plane):
        return pltpu.make_async_remote_copy(
            squares.at[layer, me, part(g)], squares.at[layer, me, part(g)],
            sq_send.at[layer, g], sq_recv.at[layer, g],
            device_id=(partner(c, d), plane), device_id_type=MESH,
        )

    def sq_wait(sem, layer, g):
        drain(squares.at[layer, pl.ds(0, len(peers)), part(g)], sem.at[layer, g])

    def w_pieces(layer, q):
        return [
            (folded_maps.at[q, pl.ds(0, dim)], weights.at[layer, pl.ds(0, dim)]),
            (folded_maps.at[q, pl.ds(dim, dim)], weights.at[layer, pl.ds(dim, dim)]),
            (gain_out.at[q], gains.at[layer]),
        ]

    def w_copy(layer, to, i):
        source, target = w_pieces(layer, to % 2)[i]
        return pltpu.make_async_remote_copy(
            source, target, w_send.at[to, i], w_recv.at[layer, i],
            device_id=(c, to), device_id_type=MESH,
        )

    def send_weights(layer, *targets):
        for i in range(3):
            for to in targets:
                w_copy(layer, to, i).start()

    def weights_sent(layer, *targets):
        for to in targets:
            for i in range(3):
                w_copy(layer, to, i).wait_send()

    def await_piece(layer, i):
        source, target = w_pieces(layer, 0)[i]
        pltpu.make_async_remote_copy(
            source, target, w_send.at[0, i], w_recv.at[layer, i],
            device_id=(c, other), device_id_type=MESH,
        ).wait_recv()

    @pl.when(z == 0)
    def _():
        send_weights(0, 3, 2)

    for d in FAR_FIRST:
        tok_copy(d).start()
    for d in FAR_FIRST:
        first_sq_copy(d).start()
    pl.semaphore_signal(ready_sem, 1, device_id=(c, other), device_id_type=MESH)

    @pl.when(z > 0)
    def _():
        fold()

    for layer, to in ((1, 0), (2, 3), (3, 2)):
        @pl.when(z == layer)
        def _():
            send_weights(layer, to)

    at_row = lax.broadcasted_iota(jnp.int32, (tokens, tokens), 0)
    at_col = lax.broadcasted_iota(jnp.int32, (tokens, tokens), 1)
    causal = at_row <= at_col

    def out_copy(slot, plane, block):
        return pltpu.make_async_remote_copy(
            stream.at[slot, rows(block)], out_ref.at[0, 0, :, cols(me)],
            out_send.at[slot], out_recv.at[0],
            device_id=(block, plane), device_id_type=MESH,
        )

    def own_out(slot):
        return pltpu.make_async_copy(
            stream.at[slot, rows(c)], out_ref.at[0, 0, :, cols(me)], local_sem.at[0]
        )

    def send_out(slot, plane, blocks):
        for block in reversed(blocks):
            mine = jnp.logical_and(c == block, z == plane)

            @pl.when(jnp.logical_not(mine))
            def _():
                out_copy(slot, plane, block).start()

            @pl.when(mine)
            def _():
                own_out(slot).start()

    def attend(slot, block, exact, fine):
        queries = exact.astype(jnp.bfloat16)
        right[block, tokens:] = queries
        scores = product(stream[slot, rows(block)], queries)
        if fine:
            rest = (exact - queries.astype(jnp.float32)).astype(jnp.bfloat16)
            scores = scores + product(stream[slot, rows(block)], rest)
        right[block, :tokens] = jnp.where(causal, scores, 0.0).astype(jnp.bfloat16)

    def pair_of(pair):
        return jnp.concatenate([turned[2 * pair], turned[2 * pair + 1]], 1)

    def project(layer, slot, pair):
        projected = product(weights[layer], pair_of(pair))
        for i in range(2):
            here = projected[:, i * tokens : (i + 1) * tokens]
            left[2 * pair + i] = here[dim:]
            attend(slot, 2 * pair + i, here[:dim], pair + i == 0)

    def turn(block):
        turned[block] = stream[0, rows(block)].T

    def attend_first(block):
        attend(0, block, product(weights[0, :dim], turned[block]), False)

    def spread_gains(layer):
        gain_cols[...] = lanes_to_rows(gains[layer])

    def mix(layer, g):
        first = sum(GROUPS[:g])
        span = GROUPS[g]
        slot = lax.rem(layer, 2)

        @pl.when(layer > 0)
        def _():
            sq_wait(sq_recv, layer, g)

        mean = jnp.sum(squares[layer, :, first : first + span], 0) * (1.0 / features)
        scale = lax.rsqrt(mean + epsilon)
        twice = scale * scale
        sums = []
        running = state[...] if g else jnp.zeros((dim, dim), jnp.float32)
        for i in range(span):
            block = first + i
            own_scale, own_twice = scale[i : i + 1], twice[i : i + 1]
            scaled = (left[block] * own_twice).astype(jnp.bfloat16)
            mixed = product(
                jnp.concatenate([scaled, running.astype(jnp.bfloat16)], 1), right[block]
            )
            if block + 1 < ctx_size:
                running = running + product(scaled, stream[slot, rows(block)])
            power = jnp.sum(mixed * mixed, 0, keepdims=True) * (1.0 / dim)
            factor = own_scale * lax.rsqrt(own_twice * power + epsilon)
            leaving = turned[block].astype(jnp.float32) + gain_cols[...] * (mixed * factor)
            rounded = leaving.astype(jnp.bfloat16)
            turned[block] = rounded
            stream[1 - slot, rows(block)] = rounded.T
            sums.append(jnp.sum(leaving * leaving, 0, keepdims=True))
        if g + 1 < len(GROUPS):
            state[...] = running
        squares[layer + 1, me, first : first + span] = jnp.concatenate(sums, 0)

        @pl.when(layer < top)
        def _():
            for d, plane in peers:
                sq_copy(layer + 1, g, d, plane).start()

        @pl.when(layer == top)
        def _():
            send_out(0, top, range(first, first + span))

        if g + 1 == len(GROUPS):
            @pl.when(layer == base)
            def _():
                send_out(1, base, range(ctx_size))

    @pl.when(z == 1)
    def _():
        send_weights(1, 3, 2)

    @pl.when(z == 0)
    def _():
        weights_sent(0, 3, 2)
        send_weights(0, 1)

    def await_first(i):
        @pl.when(z > 0)
        def _():
            await_piece(0, i)

    def arrive(pair):
        for d in pair:
            tok_copy(d).wait_recv()
        for d in pair:
            turn(partner(c, d))

    local[1].wait()
    turn(c)
    arrive((1,))
    arrive((6, 7))
    await_first(0)
    for d in (0, 1, 6, 7):
        attend_first(partner(c, d))
    for pair in ((2, 4), (3, 5)):
        arrive(pair)
        for d in pair:
            attend_first(partner(c, d))
    await_first(1)
    attend(0, 0, product(weights[0, :dim], turned[0]), True)
    for pair in range(ctx_size // 2):
        values = product(weights[0, dim:], pair_of(pair))
        for i in range(2):
            left[2 * pair + i] = values[:, i * tokens : (i + 1) * tokens]
    await_first(2)
    spread_gains(0)

    first_sq_wait(sq_recv)
    pl.semaphore_wait(ready_sem, 1)

    def one_layer(layer, carry):
        for g in range(len(GROUPS)):
            mix(layer, g)

        @pl.when(layer < top)
        def _():
            @pl.when(layer + 1 != z)
            def _():
                for i in range(3):
                    await_piece(layer + 1, i)

            spread_gains(layer + 1)
            for pair in range(ctx_size // 2):
                project(layer + 1, lax.rem(layer + 1, 2), pair)

        @pl.when(layer > 0)
        def _():
            for g in range(len(GROUPS)):
                sq_wait(sq_send, layer, g)

        return carry

    lax.fori_loop(0, base + 2, one_layer, 0)

    first_sq_wait(sq_send)
    drain(stream.at[0, pl.ds(0, (ctx_size - 1) * tokens)], tok_send.at[0])
    for layer, targets in ((0, (1,)), (1, (3, 2, 0)), (2, (3,)), (3, (2,))):
        @pl.when(z == layer)
        def _():
            weights_sent(layer, *targets)

    for slot, plane in ((1, base), (0, top)):
        @pl.when(z == plane)
        def _():
            drain(stream.at[slot, pl.ds(0, (ctx_size - 1) * tokens)], out_send.at[slot])
            own_out(slot).wait()

        @pl.when(z != plane)
        def _():
            drain(stream.at[slot], out_send.at[slot])

    drain(out_ref.at[0, 0, :, pl.ds(0, len(peers) * dim)], out_recv.at[0])


def relay(tokens, w_qkv, norm_gain, out_gain):
    ctx_size, sections = lax.axis_size("ctx"), lax.axis_size("pipe")
    rows, features = tokens.shape[1:]
    dim = w_qkv.shape[2]
    length = ctx_size * rows
    dma = pltpu.SemaphoreType.DMA
    return pl.pallas_call(
        functools.partial(relay_kernel, (ctx_size, sections, dim, rows)),
        out_shape=pltpu.VMEM((1,) + tokens.shape, jnp.bfloat16),
        in_specs=[pl.BlockSpec(memory_space=pl.ANY)] * 4,
        out_specs=pl.BlockSpec(memory_space=pltpu.VMEM),
        scratch_shapes=[
            pltpu.VMEM((rows, features), jnp.bfloat16),
            pltpu.VMEM((2, length, dim), jnp.bfloat16),
            pltpu.VMEM((ctx_size, dim, rows), jnp.bfloat16),
            pltpu.VMEM((2, dim, 3 * dim), jnp.bfloat16),
            pltpu.VMEM((2, 1, dim), jnp.float32),
            pltpu.VMEM((2, 1, dim), jnp.float32),
            pltpu.VMEM((2, 2 * dim, dim), jnp.bfloat16),
            pltpu.VMEM((sections, 2 * dim, dim), jnp.bfloat16),
            pltpu.VMEM((sections, 1, dim), jnp.float32),
            pltpu.VMEM((dim, rows), jnp.float32),
            pltpu.VMEM((ctx_size, dim, rows), jnp.float32),
            pltpu.VMEM((ctx_size, rows + dim, rows), jnp.bfloat16),
            pltpu.VMEM((dim, dim), jnp.float32),
            pltpu.VMEM((sections + 1, 2 * ctx_size, ctx_size, rows), jnp.float32),
            pltpu.SemaphoreType.REGULAR,
            dma((8,)),
            dma((1,)),
            dma((ctx_size,)),
            dma((sections, len(GROUPS))),
            dma((sections, len(GROUPS))),
            dma((sections, 3)),
            dma((sections, 3)),
            dma((2,)),
            dma((1,)),
        ],
        compiler_params=pltpu.CompilerParams(collective_id=0, has_side_effects=True),
    )(tokens, w_qkv, norm_gain, out_gain)


def solution(mesh):
    ctx_size, sections = mesh.shape["ctx"], mesh.shape["pipe"]

    def body(tokens, w_qkv, norm_gain, out_gain):
        micro_count, rows = tokens.shape[:2]
        fits = (
            ctx_size == 8
            and sections == 4
            and micro_count == 1
            and rows == 128
            and w_qkv.shape[1] == 2 * ctx_size
            and w_qkv.shape[2] == 128
        )
        return (relay if fits else shards)(tokens, w_qkv, norm_gain, out_gain)

    placed = (P(None, "ctx", None), P("pipe", None, None, None), P("pipe", None), P("pipe", None))
    return jax.shard_map(
        body, mesh=mesh, in_specs=placed, out_specs=P("pipe", None, "ctx", None), check_vma=False
    )
```

```python
import functools

import jax
import jax.numpy as jnp
from jax import lax
from jax.experimental import pallas as pl
from jax.experimental.pallas import tpu as pltpu
from jax.sharding import PartitionSpec as P

epsilon = 1e-06


def shifted(block, axis, distance):
    devices = range(lax.axis_size(axis))
    route = [(i - distance, i) for i in devices if i - distance in devices]
    return lax.ppermute(block, axis, route)


def run_layer(stream, gain_in, weights, gain_out):
    row_count = stream.shape[0]
    head_count = weights.shape[0]
    head_dim = weights.shape[1]
    widened = stream.astype(jnp.float32)
    normed = (
        widened * lax.rsqrt(jnp.mean(widened * widened, -1, keepdims=True) + epsilon) * gain_in
    ).astype(jnp.bfloat16)
    projected = jnp.einsum(
        "thd,hde->hte",
        normed.reshape(row_count, head_count, head_dim),
        weights,
        preferred_element_type=jnp.float32,
    )
    queries = (projected[..., :head_dim] * head_dim ** (-0.5)).astype(jnp.bfloat16)
    keys_local = projected[..., head_dim : 2 * head_dim].astype(jnp.bfloat16)
    values_local = projected[..., 2 * head_dim :].astype(jnp.bfloat16)
    kv_state = jnp.einsum(
        "hte,htf->hef", keys_local, values_local, preferred_element_type=jnp.float32
    )
    flat_state = kv_state.reshape(1, head_count * head_dim, head_dim)
    spread = lax.all_to_all(
        flat_state.astype(jnp.bfloat16), "ctx", split_axis=1, concat_axis=0, tiled=True
    ).astype(flat_state.dtype)
    running = jnp.cumsum(spread, axis=0)
    lower = jnp.concatenate([jnp.zeros_like(spread[:1]), running[:-1]], axis=0)
    returned = lax.all_to_all(
        lower.astype(jnp.bfloat16), "ctx", split_axis=0, concat_axis=1, tiled=True
    ).astype(lower.dtype)
    prefix = returned.reshape(kv_state.shape)
    scores = jnp.einsum("hte,hse->hts", queries, keys_local, preferred_element_type=jnp.float32)
    positions = jnp.arange(row_count, dtype=jnp.int32)
    causal = positions[:, None] >= positions[None, :]
    masked = jnp.where(causal, scores, 0.0).astype(jnp.bfloat16)
    mixed_heads = jnp.einsum(
        "hts,hsf->htf", masked, values_local, preferred_element_type=jnp.float32
    )
    mixed_heads = mixed_heads + jnp.einsum(
        "hte,hef->htf", queries, prefix.astype(jnp.bfloat16), preferred_element_type=jnp.float32
    )
    mixed_heads = mixed_heads * lax.rsqrt(
        jnp.mean(mixed_heads * mixed_heads, -1, keepdims=True) + epsilon
    )
    branch = jnp.transpose(mixed_heads, (1, 0, 2)).reshape(row_count, head_count * head_dim)
    return (widened + branch * gain_out).astype(jnp.bfloat16)


def shards(tokens, w_qkv, norm_gain, out_gain):
    section_count = lax.axis_size("pipe")
    section_index = lax.axis_index("pipe")
    micro_count = tokens.shape[0]
    hidden_buffer = jnp.zeros(tokens.shape, jnp.bfloat16)
    carried = jnp.zeros(tokens.shape[1:], jnp.bfloat16)
    total_steps = micro_count + section_count - 1
    for tick_index in range(total_steps):
        fresh = tokens[min(tick_index, micro_count - 1)]
        layer_input = jnp.where(section_index == 0, fresh, carried)
        result = run_layer(layer_input, norm_gain[0], w_qkv[0], out_gain[0])
        micro_index = tick_index - section_index
        usable = (micro_index >= 0) & (micro_index < micro_count)
        slot_index = jnp.clip(micro_index, 0, micro_count - 1)
        previous = lax.dynamic_index_in_dim(hidden_buffer, slot_index, 0, keepdims=False)
        hidden_buffer = lax.dynamic_update_index_in_dim(
            hidden_buffer, jnp.where(usable, result, previous), slot_index, 0
        )
        if tick_index + 1 < total_steps:
            carried = shifted(result, "pipe", 1)
    return hidden_buffer[None]


MESH = pl.DeviceIdType.MESH
FAR_FIRST = (6, 7, 2, 4, 3, 5, 1)


def partner(index, flips):
    total = 0
    for bit in (1, 2, 4):
        own = lax.rem(index // bit, 2)
        total = total + (lax.rem(own + 1, 2) if flips & bit else own) * bit
    return total


def lanes_to_rows(row):
    return jnp.broadcast_to(row, (128, row.shape[1])).T


def product(a, b):
    return jnp.dot(a, b, preferred_element_type=jnp.float32)


GROUPS = (1, 2, 2, 3)


def relay_kernel(
    sizes,
    tok_ref,
    w_ref,
    gin_ref,
    gout_ref,
    out_ref,
    own,
    stream,
    turned,
    raw,
    gain_in,
    gain_out,
    folded_maps,
    weights,
    gains,
    gain_cols,
    left,
    right,
    state,
    squares,
    ready_sem,
    local_sem,
    tok_send,
    tok_recv,
    sq_send,
    sq_recv,
    w_send,
    w_recv,
    out_send,
    out_recv,
):
    ctx_size, sections, dim, tokens = sizes
    features = 2 * ctx_size * dim
    c = lax.axis_index("ctx")
    z = lax.axis_index("pipe")
    side = lax.rem(z, 2)
    base = z - side
    top = base + 1
    other = base + 1 - side
    me = side * ctx_size + c

    def cols(head):
        return pl.ds(pl.multiple_of(head * dim, dim), dim)

    def rows(device):
        return pl.ds(pl.multiple_of(device * tokens, tokens), tokens)

    local = [
        pltpu.make_async_copy(tok_ref.at[0], own, local_sem.at[0]),
        pltpu.make_async_copy(tok_ref.at[0, :, cols(me)], stream.at[0, rows(c)], local_sem.at[1]),
    ]
    parts = []
    for q in range(2):
        head = q * ctx_size + c
        parts += [
            pltpu.make_async_copy(w_ref.at[0, head], raw.at[q], local_sem.at[2 + 3 * q]),
            pltpu.make_async_copy(gin_ref.at[:, cols(head)], gain_in.at[q], local_sem.at[3 + 3 * q]),
            pltpu.make_async_copy(gout_ref.at[:, cols(head)], gain_out.at[q], local_sem.at[4 + 3 * q]),
        ]
    for copy in local + parts:
        copy.start()

    peers = [(d, plane) for plane in (other, z) for d in (6, 7)]
    peers += [(d, plane) for plane in (other, z) for d in (2, 4, 3, 5)]
    peers += [(0, other), (1, other), (1, z)]
    barrier = pltpu.get_barrier_semaphore()
    for step in range(1, sections):
        plane = lax.rem(z + step, sections)
        pl.semaphore_signal(barrier, 1, device_id=(c, plane), device_id_type=MESH)
    for d in FAR_FIRST:
        pl.semaphore_signal(barrier, 1, device_id=(partner(c, d), z), device_id_type=MESH)

    def fold():
        for copy in parts:
            copy.wait()
        for q in range(2):
            across = gain_in[q]
            query = raw[q, :, :dim]
            key = raw[q, :, dim : 2 * dim]
            value = raw[q, :, 2 * dim :].astype(jnp.float32)
            crossed = lax.dot_general(
                key, query, (((1,), (1,)), ((), ())), preferred_element_type=jnp.float32
            )
            crossed = crossed * (across * dim ** (-0.5)) * lanes_to_rows(across)
            folded_maps[q, :dim] = crossed.astype(jnp.bfloat16)
            folded_maps[q, dim:] = (value.T * across).astype(jnp.bfloat16)
        weights[z] = folded_maps[side]
        gains[z] = gain_out[side]

    @pl.when(z == 0)
    def _():
        fold()

    local[0].wait()
    folded = jnp.zeros((tokens, 128), jnp.float32)
    for i in range(features // 128):
        piece = own[:, i * 128 : (i + 1) * 128].astype(jnp.float32)
        folded = folded + piece * piece
    total = jnp.sum(folded.T, 0, keepdims=True)
    which = lax.broadcasted_iota(jnp.int32, (ctx_size, tokens), 0)
    squares[0, me] = jnp.where(which == c, jnp.broadcast_to(total, (ctx_size, tokens)), 0.0)
    away = (1 - side) * ctx_size
    squares[0, pl.ds(away, ctx_size)] = jnp.zeros((ctx_size, ctx_size, tokens), jnp.float32)

    pl.semaphore_wait(barrier, ctx_size - 1 + sections - 1)

    def tok_copy(d):
        to = partner(c, d)
        return pltpu.make_async_remote_copy(
            tok_ref.at[0, :, cols(side * ctx_size + to)], stream.at[0, rows(c)],
            tok_send.at[0], tok_recv.at[d], device_id=(to, z), device_id_type=MESH,
        )

    def part(g):
        return pl.ds(sum(GROUPS[:g]), GROUPS[g])

    def first_sq_copy(d):
        return pltpu.make_async_remote_copy(
            squares.at[0, me], squares.at[0, me], sq_send.at[0, 0], sq_recv.at[0, 0],
            device_id=(partner(c, d), z), device_id_type=MESH,
        )

    def drain(every, sem):
        pltpu.make_async_copy(every, every, sem).wait()

    def first_sq_wait(sem):
        drain(squares.at[0, pl.ds(0, ctx_size - 1)], sem.at[0, 0])

    def sq_copy(layer, g, d, plane):
        return pltpu.make_async_remote_copy(
            squares.at[layer, me, part(g)], squares.at[layer, me, part(g)],
            sq_send.at[layer, g], sq_recv.at[layer, g],
            device_id=(partner(c, d), plane), device_id_type=MESH,
        )

    def sq_wait(sem, layer, g):
        drain(squares.at[layer, pl.ds(0, len(peers)), part(g)], sem.at[layer, g])

    def w_pieces(layer, q):
        return [
            (folded_maps.at[q, pl.ds(0, dim)], weights.at[layer, pl.ds(0, dim)]),
            (folded_maps.at[q, pl.ds(dim, dim)], weights.at[layer, pl.ds(dim, dim)]),
            (gain_out.at[q], gains.at[layer]),
        ]

    def w_copy(layer, to, i):
        source, target = w_pieces(layer, to % 2)[i]
        return pltpu.make_async_remote_copy(
            source, target, w_send.at[to, i], w_recv.at[layer, i],
            device_id=(c, to), device_id_type=MESH,
        )

    def send_weights(layer, *targets):
        for i in range(3):
            for to in targets:
                w_copy(layer, to, i).start()

    def weights_sent(layer, *targets):
        for to in targets:
            for i in range(3):
                w_copy(layer, to, i).wait_send()

    def await_piece(layer, i):
        source, target = w_pieces(layer, 0)[i]
        pltpu.make_async_remote_copy(
            source, target, w_send.at[0, i], w_recv.at[layer, i],
            device_id=(c, other), device_id_type=MESH,
        ).wait_recv()

    @pl.when(z == 0)
    def _():
        send_weights(0, 3, 2)

    for d in FAR_FIRST:
        tok_copy(d).start()
    for d in FAR_FIRST:
        first_sq_copy(d).start()
    pl.semaphore_signal(ready_sem, 1, device_id=(c, other), device_id_type=MESH)

    @pl.when(z > 0)
    def _():
        fold()

    for layer, to in ((2, 3), (3, 2)):
        @pl.when(z == layer)
        def _():
            send_weights(layer, to)

    at_row = lax.broadcasted_iota(jnp.int32, (tokens, tokens), 0)
    at_col = lax.broadcasted_iota(jnp.int32, (tokens, tokens), 1)
    causal = at_row <= at_col

    def out_copy(slot, plane, block):
        return pltpu.make_async_remote_copy(
            stream.at[slot, rows(block)], out_ref.at[0, 0, :, cols(me)],
            out_send.at[slot], out_recv.at[0],
            device_id=(block, plane), device_id_type=MESH,
        )

    def own_out(slot):
        return pltpu.make_async_copy(
            stream.at[slot, rows(c)], out_ref.at[0, 0, :, cols(me)], local_sem.at[0]
        )

    def send_out(slot, plane, blocks):
        for block in reversed(blocks):
            mine = jnp.logical_and(c == block, z == plane)

            @pl.when(jnp.logical_not(mine))
            def _():
                out_copy(slot, plane, block).start()

            @pl.when(mine)
            def _():
                own_out(slot).start()

    def attend(slot, block, exact, fine):
        queries = exact.astype(jnp.bfloat16)
        right[block, tokens:] = queries
        scores = product(stream[slot, rows(block)], queries)
        if fine:
            rest = (exact - queries.astype(jnp.float32)).astype(jnp.bfloat16)
            scores = scores + product(stream[slot, rows(block)], rest)
        right[block, :tokens] = jnp.where(causal, scores, 0.0).astype(jnp.bfloat16)

    def pair_of(pair):
        return jnp.concatenate([turned[2 * pair], turned[2 * pair + 1]], 1)

    def project(layer, slot, pair):
        projected = product(weights[layer], pair_of(pair))
        for i in range(2):
            here = projected[:, i * tokens : (i + 1) * tokens]
            left[2 * pair + i] = here[dim:]
            attend(slot, 2 * pair + i, here[:dim], pair + i == 0)

    def turn(block):
        turned[block] = stream[0, rows(block)].T

    def attend_first(block):
        attend(0, block, product(weights[0, :dim], turned[block]), False)

    def spread_gains(layer):
        gain_cols[...] = lanes_to_rows(gains[layer])

    def mix(layer, g):
        first = sum(GROUPS[:g])
        span = GROUPS[g]
        slot = lax.rem(layer, 2)

        @pl.when(layer > 0)
        def _():
            sq_wait(sq_recv, layer, g)

        mean = jnp.sum(squares[layer, :, first : first + span], 0) * (1.0 / features)
        scale = lax.rsqrt(mean + epsilon)
        twice = scale * scale
        sums = []
        running = state[...] if g else jnp.zeros((dim, dim), jnp.float32)
        for i in range(span):
            block = first + i
            own_scale, own_twice = scale[i : i + 1], twice[i : i + 1]
            scaled = (left[block] * own_twice).astype(jnp.bfloat16)
            mixed = product(
                jnp.concatenate([scaled, running.astype(jnp.bfloat16)], 1), right[block]
            )
            if block + 1 < ctx_size:
                running = running + product(scaled, stream[slot, rows(block)])
            power = jnp.sum(mixed * mixed, 0, keepdims=True) * (1.0 / dim)
            factor = own_scale * lax.rsqrt(own_twice * power + epsilon)
            leaving = turned[block].astype(jnp.float32) + gain_cols[...] * (mixed * factor)
            rounded = leaving.astype(jnp.bfloat16)
            turned[block] = rounded
            stream[1 - slot, rows(block)] = rounded.T
            sums.append(jnp.sum(leaving * leaving, 0, keepdims=True))
        if g + 1 < len(GROUPS):
            state[...] = running
        squares[layer + 1, me, first : first + span] = jnp.concatenate(sums, 0)

        @pl.when(layer < top)
        def _():
            for d, plane in peers:
                sq_copy(layer + 1, g, d, plane).start()

        @pl.when(layer == top)
        def _():
            send_out(0, top, range(first, first + span))

        if g + 1 == len(GROUPS):
            @pl.when(layer == base)
            def _():
                send_out(1, base, range(ctx_size))

    @pl.when(z == 1)
    def _():
        send_weights(1, 3, 2)
        send_weights(1, 0)

    @pl.when(z == 0)
    def _():
        weights_sent(0, 3, 2)
        send_weights(0, 1)

    def await_first(i):
        @pl.when(z > 0)
        def _():
            await_piece(0, i)

    def arrive(pair):
        for d in pair:
            tok_copy(d).wait_recv()
        for d in pair:
            turn(partner(c, d))

    local[1].wait()
    turn(c)
    arrive((1,))
    arrive((6, 7))
    await_first(0)
    for d in (0, 1, 6, 7):
        attend_first(partner(c, d))
    for pair in ((2, 4), (3, 5)):
        arrive(pair)
        for d in pair:
            attend_first(partner(c, d))
    await_first(1)
    attend(0, 0, product(weights[0, :dim], turned[0]), True)
    for pair in range(ctx_size // 2):
        values = product(weights[0, dim:], pair_of(pair))
        for i in range(2):
            left[2 * pair + i] = values[:, i * tokens : (i + 1) * tokens]
    await_first(2)
    spread_gains(0)

    first_sq_wait(sq_recv)
    pl.semaphore_wait(ready_sem, 1)

    def one_layer(layer, carry):
        for g in range(len(GROUPS)):
            mix(layer, g)

        @pl.when(layer < top)
        def _():
            @pl.when(layer + 1 != z)
            def _():
                for i in range(3):
                    await_piece(layer + 1, i)

            spread_gains(layer + 1)
            for pair in range(ctx_size // 2):
                project(layer + 1, lax.rem(layer + 1, 2), pair)

        @pl.when(layer > 0)
        def _():
            for g in range(len(GROUPS)):
                sq_wait(sq_send, layer, g)

        return carry

    lax.fori_loop(0, base + 2, one_layer, 0)

    first_sq_wait(sq_send)
    drain(stream.at[0, pl.ds(0, (ctx_size - 1) * tokens)], tok_send.at[0])
    for layer, targets in ((0, (1,)), (1, (3, 2, 0)), (2, (3,)), (3, (2,))):
        @pl.when(z == layer)
        def _():
            weights_sent(layer, *targets)

    for slot, plane in ((1, base), (0, top)):
        @pl.when(z == plane)
        def _():
            drain(stream.at[slot, pl.ds(0, (ctx_size - 1) * tokens)], out_send.at[slot])
            own_out(slot).wait()

        @pl.when(z != plane)
        def _():
            drain(stream.at[slot], out_send.at[slot])

    drain(out_ref.at[0, 0, :, pl.ds(0, len(peers) * dim)], out_recv.at[0])


def relay(tokens, w_qkv, norm_gain, out_gain):
    ctx_size, sections = lax.axis_size("ctx"), lax.axis_size("pipe")
    rows, features = tokens.shape[1:]
    dim = w_qkv.shape[2]
    length = ctx_size * rows
    dma = pltpu.SemaphoreType.DMA
    return pl.pallas_call(
        functools.partial(relay_kernel, (ctx_size, sections, dim, rows)),
        out_shape=pltpu.VMEM((1,) + tokens.shape, jnp.bfloat16),
        in_specs=[pl.BlockSpec(memory_space=pl.ANY)] * 4,
        out_specs=pl.BlockSpec(memory_space=pltpu.VMEM),
        scratch_shapes=[
            pltpu.VMEM((rows, features), jnp.bfloat16),
            pltpu.VMEM((2, length, dim), jnp.bfloat16),
            pltpu.VMEM((ctx_size, dim, rows), jnp.bfloat16),
            pltpu.VMEM((2, dim, 3 * dim), jnp.bfloat16),
            pltpu.VMEM((2, 1, dim), jnp.float32),
            pltpu.VMEM((2, 1, dim), jnp.float32),
            pltpu.VMEM((2, 2 * dim, dim), jnp.bfloat16),
            pltpu.VMEM((sections, 2 * dim, dim), jnp.bfloat16),
            pltpu.VMEM((sections, 1, dim), jnp.float32),
            pltpu.VMEM((dim, rows), jnp.float32),
            pltpu.VMEM((ctx_size, dim, rows), jnp.float32),
            pltpu.VMEM((ctx_size, rows + dim, rows), jnp.bfloat16),
            pltpu.VMEM((dim, dim), jnp.float32),
            pltpu.VMEM((sections + 1, 2 * ctx_size, ctx_size, rows), jnp.float32),
            pltpu.SemaphoreType.REGULAR,
            dma((8,)),
            dma((1,)),
            dma((ctx_size,)),
            dma((sections, len(GROUPS))),
            dma((sections, len(GROUPS))),
            dma((sections, 3)),
            dma((sections, 3)),
            dma((2,)),
            dma((1,)),
        ],
        compiler_params=pltpu.CompilerParams(collective_id=0, has_side_effects=True),
    )(tokens, w_qkv, norm_gain, out_gain)


def solution(mesh):
    ctx_size, sections = mesh.shape["ctx"], mesh.shape["pipe"]

    def body(tokens, w_qkv, norm_gain, out_gain):
        micro_count, rows = tokens.shape[:2]
        fits = (
            ctx_size == 8
            and sections == 4
            and micro_count == 1
            and rows == 128
            and w_qkv.shape[1] == 2 * ctx_size
            and w_qkv.shape[2] == 128
        )
        return (relay if fits else shards)(tokens, w_qkv, norm_gain, out_gain)

    placed = (P(None, "ctx", None), P("pipe", None, None, None), P("pipe", None), P("pipe", None))
    return jax.shard_map(
        body, mesh=mesh, in_specs=placed, out_specs=P("pipe", None, "ctx", None), check_vma=False
    )
```
